32 devices in a mesh: order: 4 (over z), degree: 2 (over y), site: 4 (over x, core).
Axes of the slice: x: 2, y: 2, z: 4, core: 2. Of those that a mesh axis runs over, the one named last changes fastest.
Arguments:
- scene_coeffs: bfloat16 [2, 16, 128, 256, 32], P(None, None, 'degree', 'order'), may hold values from -3 to 3
- site_ids: int32 [4], P('site'), may hold values from 0 to 31
- gripper_coeffs: bfloat16 [2, 16, 128, 256], P(None, None, 'degree', 'order'), may hold values from -3 to 3
- order_table: int32 [256], replicated, may hold values from 0 to 255, each once
- wigner: bfloat16 [128, 8, 256, 256], P('degree', None, 'order'), may hold values from -0.0029907227 to 0.0029907227
Outputs:
- scores: float32 [4, 8, 256, 256], P('site', 'degree', 'order')
The draws below stay inside these ranges and needn't reach their ends.
Inputs may be any that keep to these rules, and one draw needn't show every extreme that they name: A permutation of the 256 slots; slot j holds order order_table[j] - 128. `site_ids`: sites may share a candidate.
All inputs are finite; a program needn't handle non-finite values.
Results may differ from the reference program's by a relative error of at most 0.0029.
Values may be sent and summed in bfloat16 or wider, within the bound.
A program may use at most 128 MiB of HBM per device.

```python
import math
import jax
import jax.numpy as jnp
from jax import lax

B = 128
C = 16
CAND = 32
NB = 8
SITES = 4
SLOTS = 256
GRID = 256


def touch_ends(result, own_key, least, largest):
    shape = result.shape
    spot = [jax.random.randint(jax.random.fold_in(own_key, axis), (), 0, shape[axis]) for axis in range(len(shape))]
    result = result.at[tuple(spot)].set(least)
    longest = shape.index(max(shape))
    spot[longest] = (spot[longest] + 1) % shape[longest]
    return result.at[tuple(spot)].set(largest)


def level_of(key, shape, cuts, low, high):
    gain, own = 1.0, jax.random.fold_in(key, 6)
    for position, blocks in cuts:
        heights = jnp.exp(jax.random.uniform(jax.random.fold_in(own, position), (blocks,), jnp.float32, low / len(cuts), high / len(cuts)))
        gain = gain * jnp.repeat(heights, shape[position] // blocks).reshape([-1 if axis == position else 1 for axis in range(len(shape))])
    return gain


def scatter_about(rng, dims, spread, limit, pieces=(), held_as=jnp.bfloat16):
    gain = level_of(rng, dims, pieces, -0.22, 0.18) if pieces else 1.0
    array = jax.random.normal(rng, dims, jnp.float32) * spread * gain
    return jnp.minimum(jnp.maximum(array, -limit), limit).astype(held_as)


def setup_inputs(seed: int = 0) -> dict:
    splits = jax.random.split(jax.random.key(seed), 6)
    return {
        "scene_coeffs": scatter_about(splits[0], (2, C, B, SLOTS, CAND), 0.5, 3.0, ((2, 2), (3, 4))),
        "site_ids": touch_ends(jax.random.randint(splits[1], (SITES,), 0, CAND), jax.random.fold_in(splits[1], 1), 0, CAND - 1).astype(jnp.int32),
        "gripper_coeffs": scatter_about(splits[2], (2, C, B, SLOTS), 0.5, 3.0, ((2, 2), (3, 4))),
        "order_table": jax.random.permutation(splits[3], SLOTS).astype(jnp.int32),
        "wigner": scatter_about(splits[4], (B, NB, SLOTS, SLOTS), 0.0005, 0.0029907227, ((0, 2), (2, 4))),
    }


def phase_tables(order_table):
    orders = order_table.astype(jnp.int32) - B
    angles = jnp.arange(GRID, dtype=jnp.int32)
    phase_index = jnp.mod(orders[:, None] * angles[None, :], GRID)
    radians = phase_index.astype(jnp.float32) * (2.0 * math.pi / GRID)
    return orders, jnp.cos(radians), jnp.sin(radians)


def reference(scene_coeffs, site_ids, gripper_coeffs, order_table, wigner):
    orders, cosine, sine_table = phase_tables(order_table)
    magnitude = jnp.abs(orders)
    chosen = jnp.take(scene_coeffs, site_ids.astype(jnp.int32), axis=4).astype(jnp.float32)
    gripper = gripper_coeffs.astype(jnp.float32)

    def one_degree(carried, inputs):
        scene_part, grip_part, wigner_part, degree = inputs
        real_part = jnp.einsum("cms,cp->spm", scene_part[0], grip_part[0]) + jnp.einsum("cms,cp->spm", scene_part[1], grip_part[1])
        imag_part = jnp.einsum("cms,cp->spm", scene_part[1], grip_part[0]) - jnp.einsum("cms,cp->spm", scene_part[0], grip_part[1])
        permitted_mask = (magnitude[:, None] <= degree) & (magnitude[None, :] <= degree)
        product = jnp.where(permitted_mask[None, None], jnp.stack([real_part, imag_part]), jnp.float32(0.0))
        product = lax.optimization_barrier(product.astype(jnp.bfloat16)).astype(jnp.float32)
        weights = wigner_part.astype(jnp.float32)
        return carried + jnp.einsum("xspm,bpm->xsbpm", product, weights), None

    initial = jnp.zeros((2, SITES, NB, SLOTS, SLOTS), jnp.float32)
    inputs = (jnp.moveaxis(chosen, 2, 0), jnp.moveaxis(gripper, 2, 0), wigner, jnp.arange(B, dtype=jnp.int32))
    summed, _ = lax.scan(one_degree, initial, inputs)
    highest = lax.Precision.HIGHEST
    real_alpha = jnp.einsum("sbpm,mj->sbpj", summed[0], cosine, precision=highest) - jnp.einsum("sbpm,mj->sbpj", summed[1], sine_table, precision=highest)
    imag_alpha = jnp.einsum("sbpm,mj->sbpj", summed[0], sine_table, precision=highest) + jnp.einsum("sbpm,mj->sbpj", summed[1], cosine, precision=highest)
    scores = jnp.einsum("sbpj,pk->sbjk", real_alpha, cosine, precision=highest) - jnp.einsum("sbpj,pk->sbjk", imag_alpha, sine_table, precision=highest)
    return scores
```

```python
import math

import jax
import jax.numpy as jnp
from jax import lax
from jax.experimental import pallas as pl
from jax.experimental.pallas import tpu as pltpu
from jax.sharding import PartitionSpec as P


def general_shards(scene_coeffs, site_ids, gripper_coeffs, order_table, wigner):
    highest = lax.Precision.HIGHEST
    slot_count = order_table.shape[0]
    local_deg = gripper_coeffs.shape[2]
    local_ord = gripper_coeffs.shape[3]
    cand_count = scene_coeffs.shape[4]
    site_count = site_ids.shape[0]
    order_pos = lax.axis_index("order")
    degree_pos = lax.axis_index("degree")
    orders = order_table - slot_count // 2
    angles = jnp.arange(slot_count, dtype=jnp.int32)
    phase_index = jnp.mod(orders[:, None] * angles[None, :], slot_count)
    radians = phase_index.astype(jnp.float32) * (2.0 * math.pi / slot_count)
    cosine = jnp.cos(radians)
    sine_table = jnp.sin(radians)
    magnitude = jnp.abs(orders)
    resident_degrees = degree_pos * local_deg + jnp.arange(local_deg, dtype=jnp.int32)
    owned_orders = lax.dynamic_slice_in_dim(magnitude, order_pos * local_ord, local_ord)
    grip_allowed = owned_orders[None, :] <= resident_degrees[:, None]
    selector = (jnp.arange(cand_count, dtype=jnp.int32)[:, None] == site_ids[None, :]).astype(
        jnp.bfloat16
    )
    chosen = jnp.dot(
        scene_coeffs.reshape(-1, cand_count), selector, preferred_element_type=jnp.float32
    )
    chosen = chosen.astype(jnp.bfloat16).reshape(
        2, scene_coeffs.shape[1], local_deg, local_ord, site_count
    )
    grip_real = jnp.concatenate([gripper_coeffs[0], gripper_coeffs[1]], axis=0)
    grip_imag = jnp.concatenate([-gripper_coeffs[1], gripper_coeffs[0]], axis=0)
    gripper_couple = jnp.stack([grip_real, grip_imag])
    columns_in = lax.all_gather(chosen, "order", axis=3, tiled=True)
    scene_joined = jnp.concatenate([columns_in[0], columns_in[1]], axis=0)
    product = jnp.einsum(
        "aonw,iaob->iobnw", scene_joined, gripper_couple, preferred_element_type=jnp.float32
    )
    permitted_mask = grip_allowed[:, :, None] & (
        magnitude[None, None, :] <= resident_degrees[:, None, None]
    )
    product = jnp.where(permitted_mask[None, :, :, :, None], product, jnp.float32(0.0)).astype(
        jnp.bfloat16
    )
    partial_value = jnp.einsum(
        "ylprs,lbpr->ysbpr", product, wigner, preferred_element_type=jnp.float32
    )
    summed = lax.psum_scatter(partial_value, "degree", scatter_dimension=2, tiled=True)
    phase_pair = jnp.concatenate([cosine, sine_table], axis=1)
    products = jnp.einsum(
        "xsbpm,mk->xsbpk", summed, phase_pair, precision=highest, preferred_element_type=jnp.float32
    )
    real_alpha = products[0, ..., :slot_count] - products[1, ..., slot_count:]
    imag_alpha = products[0, ..., slot_count:] + products[1, ..., :slot_count]
    stacked_parts = jnp.stack([real_alpha, imag_alpha])
    exchanged = lax.all_to_all(stacked_parts, "order", split_axis=4, concat_axis=3, tiled=True)
    first_term = jnp.einsum(
        "sbpa,pk->sbak", exchanged[0], cosine, precision=highest, preferred_element_type=jnp.float32
    )
    latter_addend = jnp.einsum(
        "sbpa,pk->sbak",
        exchanged[1],
        sine_table,
        precision=highest,
        preferred_element_type=jnp.float32,
    )
    return first_term - latter_addend


MESH = pl.DeviceIdType.MESH
F32, BF16 = jnp.float32, jnp.bfloat16
CHUNKS = 4
ROWS = 16
GROUP = 8


def cos_of(index, count):
    centred = jnp.bitwise_and(index + count // 2, count - 1) - count // 2
    half = centred.astype(F32) * F32(math.pi / count)
    sq = half * half
    poly = F32(-1.0 / 39916800.0)
    for coefficient in (1.0 / 362880.0, -1.0 / 5040.0, 1.0 / 120.0, -1.0 / 6.0, 1.0):
        poly = poly * sq + F32(coefficient)
    sine = poly * half
    return 1.0 - 2.0 * sine * sine


def split(value):
    high = value.astype(BF16)
    return high, (value - high.astype(F32)).astype(BF16)


def fused_kernel(
    scene_ref, site_ref, g_hbm, row_hbm, w_ref, out_ref, wbuf, *scratch
):
    cands, scratch = scratch[:CHUNKS], scratch[CHUNKS:]
    fused_body(scene_ref, site_ref, g_hbm, row_hbm, w_ref, out_ref, wbuf, cands, *scratch)


def fused_body(
    scene_ref, site_ref, g_hbm, row_hbm, w_ref, out_ref, wbuf, cands,
    g_ref, row_ref, sbuf, prod, accbuf, rs_send, rs_recv, a_send, a_recv, halfacc,
    alpha_hi, alpha_lo, gamma_hi, gamma_lo, g32, col,
    in_sem, c_sem, w_sem, s_send_sem, s_recv_sem, r_send_sem, r_recv_sem, x_send_sem, x_recv_sem,
):
    me = lax.axis_index("order")
    deg = lax.axis_index("degree")
    HL, NBETA, P, M = wbuf.shape[2:]
    L = 2 * HL
    SL = 2 * M
    BO = NBETA // 2
    K = scene_ref.shape[0]
    first = me // 2
    second = 1 - first
    near = first * 2 + (1 - me % 2)
    per = HL // CHUNKS
    blocks = P // ROWS

    def w_copy(h, c):
        return pltpu.make_async_copy(
            w_ref.at[:, pl.ds(c * per, per), :, :, pl.ds(pl.multiple_of(h * M, M), M)],
            wbuf.at[h, :, pl.ds(c * per, per)],
            w_sem.at[h, c],
        )

    def c_copy(c):
        return pltpu.make_async_copy(
            scene_ref.at[:, :, pl.ds(c * per, per)], cands[c], c_sem.at[c]
        )

    c_copy(0).start()
    g_copy = pltpu.make_async_copy(g_hbm, g_ref, in_sem.at[0])
    row_copy = pltpu.make_async_copy(row_hbm, row_ref, in_sem.at[1])
    row_copy.start()
    g_copy.start()
    for c in range(1, CHUNKS):
        c_copy(c).start()

    barrier = pltpu.get_barrier_semaphore()
    for off in (1, 2, 3):
        pl.semaphore_signal(barrier, 1, device_id={"order": (me + off) % 4}, device_id_type=MESH)
    pl.semaphore_signal(barrier, 1, device_id={"degree": 1 - deg}, device_id_type=MESH)

    site = site_ref[0]
    pick_row = lax.broadcasted_iota(jnp.int32, (K, K * GROUP), 0)
    pick_col = lax.broadcasted_iota(jnp.int32, (K, K * GROUP), 1)
    pick = (pick_col == pick_row * GROUP + site % GROUP).astype(F32).astype(BF16)

    def select(c):
        def step(i, carry):
            halves = []
            for part in range(2):
                tile = cands[c][:, part, i, site // GROUP].astype(F32)
                tile = tile.reshape(K * GROUP, P).astype(BF16)
                halves.append(jnp.dot(pick, tile, preferred_element_type=F32))
            sbuf[me, c * per + i] = jnp.concatenate(halves, axis=1).astype(BF16)
            return carry

        c_copy(c).wait()
        lax.fori_loop(0, per, step, 0, unroll=True)

    def hop(block, c, way):
        rows = pl.ds(c * per, per)
        return pltpu.make_async_remote_copy(
            src_ref=sbuf.at[block, rows],
            dst_ref=sbuf.at[block, rows],
            send_sem=s_send_sem.at[way, block, c], recv_sem=s_recv_sem.at[block, c],
            device_id={"order": me + 1 - 2 * way}, device_id_type=MESH,
        )

    def send_own(c):
        @pl.when(me < 3)
        def _():
            hop(me, c, 0).start()

        @pl.when(me > 0)
        def _():
            hop(me, c, 1).start()

    def prepare():
        row_copy.wait()
        for h in range(2):
            line = jnp.broadcast_to(row_ref[h].astype(F32), (M, M))
            col[h * M : (h + 1) * M, :] = jnp.transpose(line).astype(jnp.int32) - SL // 2
        g_copy.wait()
        real = g_ref[0].astype(F32).reshape(K // 2 * L, P)
        imag = g_ref[1].astype(F32).reshape(K // 2 * L, P)
        g32[: K // 2 * L] = jnp.concatenate([real, -imag], axis=1)
        g32[K // 2 * L :] = jnp.concatenate([imag, real], axis=1)
        accbuf[...] = jnp.zeros_like(accbuf)

    dims = (((0,), (0,)), ((), ()))

    def tables():
        quarter = SL // 4
        lane = lax.broadcasted_iota(jnp.int32, (M, M), 1)
        for h in range(2):
            orders = col[h * M : (h + 1) * M, :]
            for t in range(4):
                at = slice(t * M, (t + 1) * M)
                phase = orders * (t * P + lane % P)
                for x in range(2):
                    hi, lo = split(cos_of(phase + (x - lane // P) * quarter, SL))
                    alpha_hi[h, x * M : (x + 1) * M, at] = hi
                    alpha_lo[h, x * M : (x + 1) * M, at] = lo
                phase = orders * ((t % 2) * M + lane)
                hi, lo = split(cos_of(phase + (t // 2) * quarter, SL))
                gamma_hi[h * M : (h + 1) * M, at] = hi
                gamma_lo[h * M : (h + 1) * M, at] = lo

    def r_copy(h, blk):
        return pltpu.make_async_remote_copy(
            src_ref=rs_send.at[h, blk], dst_ref=rs_recv.at[h, blk],
            send_sem=r_send_sem.at[h, blk], recv_sem=r_recv_sem.at[h, blk],
            device_id={"degree": 1 - deg}, device_id_type=MESH,
        )

    def compute(h, arrivals):
        mag_p = jnp.abs(col[pl.ds(pl.multiple_of(me * P, P), P), :])
        mag_m = jnp.abs(row_ref[h] - SL // 2)
        most = jnp.maximum(mag_p, jnp.broadcast_to(mag_m, (P, M)))
        most = jnp.concatenate([most, most], axis=0)

        def chunk(c, carry):
            arrivals(c)
            for i in range(per):
                step = c * per + i
                b0, b1 = sbuf[2 * h, step], sbuf[2 * h + 1, step]
                low = jnp.concatenate([b0[:, :P], b1[:, :P]], axis=1)
                high = jnp.concatenate([b0[:, P:], b1[:, P:]], axis=1)
                for part, scene in ((0, low), (1, high)):
                    l = step + part * HL
                    grip = g32[pl.ds(l, K, stride=L), :].astype(BF16)
                    value = lax.dot_general(grip, scene, dims, preferred_element_type=F32)
                    value = jnp.where(most <= deg * L + l, value, F32(0.0))
                    prod[part, i] = value.astype(BF16)
            w_copy(h, c).wait()

            def rows(blk, carry):
                at = pl.multiple_of(blk * ROWS, ROWS)

                def degree_step(i, acc):
                    acc = list(acc)
                    for part in range(2):
                        pr = prod[part, i, pl.ds(at, ROWS), :].astype(F32)
                        pi = prod[part, i, pl.ds(at + P, ROWS), :].astype(F32)
                        for b in range(NBETA):
                            w = wbuf[h, part, c * per + i, b, pl.ds(at, ROWS), :].astype(F32)
                            acc[2 * b] += pr * w
                            acc[2 * b + 1] += pi * w
                    return tuple(acc)

                acc = tuple(accbuf[h, blk, n // 2, n % 2] for n in range(2 * NBETA))
                acc = lax.fori_loop(0, per, degree_step, acc, unroll=2)
                for n in range(2 * NBETA):
                    accbuf[h, blk, n // 2, n % 2] = acc[n]

                @pl.when(c == CHUNKS - 1)
                def _():
                    rs_send[h, blk] = accbuf[h, blk, pl.ds((1 - deg) * BO, BO)].astype(BF16)
                    r_copy(h, blk).start()

                return carry

            return lax.fori_loop(0, blocks, rows, carry)

        lax.fori_loop(0, CHUNKS, chunk, 0)

    def alpha(h, blk):
        r_copy(h, blk).wait_recv()
        total = accbuf[h, blk, pl.ds(deg * BO, BO)] + rs_recv[h, blk].astype(F32)
        total = jnp.concatenate(
            [total[:, 0].reshape(BO * ROWS, M), total[:, 1].reshape(BO * ROWS, M)], axis=1
        )
        hi, lo = split(total)
        value = jnp.dot(hi, alpha_hi[h], preferred_element_type=F32)
        value += jnp.dot(hi, alpha_lo[h], preferred_element_type=F32)
        value += jnp.dot(lo, alpha_hi[h], preferred_element_type=F32)
        return value

    across = lax.max(me - 1, 0) % 2
    middle = (me == 1) | (me == 2)
    other = me + 1 - 2 * across
    beyond = other + 1 - 2 * across

    def wait_block(block, c):
        hop(block, c, me // 3).wait_recv()

    def arrivals_first(c):
        wait_block(near, c)

        @pl.when(middle)
        def _():
            hop(near, c, across).start()
            wait_block(other, c)
            hop(other, c, 1 - across).start()

    def arrivals_second(c):
        @pl.when(middle)
        def _():
            wait_block(beyond, c)
            hop(beyond, c, 1 - across).start()

        @pl.when(jnp.logical_not(middle))
        def _():
            wait_block(second * 2, c)
            wait_block(second * 2 + 1, c)

    select(0)
    pl.semaphore_wait(barrier, 4)
    send_own(0)
    select(1)
    send_own(1)
    w_copy(first, 0).start()
    for c in range(2, CHUNKS):
        arrivals_first(c - 2)
        select(c)
        send_own(c)
        w_copy(first, c - 1).start()
    w_copy(first, CHUNKS - 1).start()
    for c in range(CHUNKS):
        w_copy(second, c).start()
    arrivals_first(CHUNKS - 2)
    prepare()
    arrivals_first(CHUNKS - 1)
    tables()
    compute(first, lambda c: None)
    compute(second, arrivals_second)

    def x_copy(target, source, blk, off):
        return pltpu.make_async_remote_copy(
            src_ref=a_send.at[target, blk], dst_ref=a_recv.at[source, blk],
            send_sem=x_send_sem.at[off, blk], recv_sem=x_recv_sem.at[off, blk],
            device_id={"order": target}, device_id_type=MESH,
        )

    for blk in range(blocks):
        halfacc[blk] = alpha(first, blk)
    for blk in range(blocks):
        value = (halfacc[blk] + alpha(second, blk)).astype(BF16)
        for t in range(4):
            a_send[t, blk] = value[:, t * M : (t + 1) * M]
        for off in (2, 1, 3):
            x_copy((me + off) % 4, me, blk, off).start()
        a_recv[me, blk] = a_send[me, blk]

    for blk in range(blocks):
        for off in (1, 3, 2):
            source = (me - off + 4) % 4
            x_copy(source, source, blk, off).wait_recv()

    score = jnp.zeros((BO * P, SL), F32)
    got = [
        jnp.concatenate(
            [a_recv[z, blk, b * ROWS : (b + 1) * ROWS, :] for z in range(4) for blk in range(blocks)],
            axis=0,
        )
        for b in range(BO)
    ]
    for x in range(2):
        left = jnp.concatenate([piece[:, x * P : (x + 1) * P] for piece in got], axis=1)
        for table in (gamma_hi, gamma_lo):
            score += lax.dot_general(
                left, table[:, x * SL : (x + 1) * SL], dims, preferred_element_type=F32
            )
    out_ref[0] = score.reshape(BO, P, SL)

    for c in range(CHUNKS):
        @pl.when(me < 3)
        def _():
            hop(me, c, 0).wait_send()

        @pl.when(me > 0)
        def _():
            hop(me, c, 1).wait_send()

        @pl.when(middle)
        def _():
            hop(near, c, across).wait_send()
            hop(other, c, 1 - across).wait_send()
            hop(beyond, c, 1 - across).wait_send()

    for blk in range(blocks):
        for off in (1, 2, 3):
            x_copy((me + off) % 4, me, blk, off).wait_send()
        r_copy(first, blk).wait_send()
        r_copy(second, blk).wait_send()


def fused_shards(scene_coeffs, site_ids, gripper_coeffs, order_table, wigner):
    L, NBETA, P, SL = wigner.shape
    M = SL // 2
    K = 2 * scene_coeffs.shape[1]
    BO = NBETA // 2
    NB = P // ROWS
    cand = scene_coeffs.shape[4]
    tall = jnp.transpose(scene_coeffs, (0, 1, 2, 4, 3))
    tall = tall.reshape(K, 2, L // 2, cand // GROUP, GROUP, P)
    vmem = pl.BlockSpec(memory_space=pltpu.VMEM)
    hbm = pl.BlockSpec(memory_space=pltpu.HBM)
    return pl.pallas_call(
        fused_kernel,
        out_shape=jax.ShapeDtypeStruct((1, BO, P, SL), F32),
        in_specs=[hbm, pl.BlockSpec(memory_space=pltpu.SMEM), hbm, hbm, hbm],
        out_specs=vmem,
        scratch_shapes=[
            pltpu.VMEM((2, 2, L // 2, NBETA, P, M), BF16),
            *[
                pltpu.VMEM((K, 2, L // 2 // CHUNKS, cand // GROUP, GROUP, P), BF16)
                for _ in range(CHUNKS)
            ],
            pltpu.VMEM((2, K // 2, L, P), BF16),
            pltpu.VMEM((2, 1, M), jnp.int32),
            pltpu.VMEM((4, L // 2, K, 2 * P), BF16),
            pltpu.VMEM((2, L // 2 // CHUNKS, 2 * P, M), BF16),
            pltpu.VMEM((2, NB, NBETA, 2, ROWS, M), F32),
            pltpu.VMEM((2, NB, BO, 2, ROWS, M), BF16),
            pltpu.VMEM((2, NB, BO, 2, ROWS, M), BF16),
            pltpu.VMEM((4, NB, BO * ROWS, M), BF16),
            pltpu.VMEM((4, NB, BO * ROWS, M), BF16),
            pltpu.VMEM((NB, BO * ROWS, 2 * SL), F32),
            pltpu.VMEM((2, 2 * M, 2 * SL), BF16),
            pltpu.VMEM((2, 2 * M, 2 * SL), BF16),
            pltpu.VMEM((SL, 2 * SL), BF16),
            pltpu.VMEM((SL, 2 * SL), BF16),
            pltpu.VMEM((K * L, 2 * P), F32),
            pltpu.VMEM((SL, M), jnp.int32),
            pltpu.SemaphoreType.DMA((2,)),
            pltpu.SemaphoreType.DMA((CHUNKS,)),
            pltpu.SemaphoreType.DMA((2, CHUNKS)),
            pltpu.SemaphoreType.DMA((2, 4, CHUNKS)),
            pltpu.SemaphoreType.DMA((4, CHUNKS)),
            pltpu.SemaphoreType.DMA((2, NB)),
            pltpu.SemaphoreType.DMA((2, NB)),
            pltpu.SemaphoreType.DMA((4, NB)),
            pltpu.SemaphoreType.DMA((4, NB)),
        ],
        compiler_params=pltpu.CompilerParams(
            collective_id=0, has_side_effects=True, vmem_limit_bytes=48 * 1024 * 1024
        ),
    )(
        tall,
        site_ids,
        gripper_coeffs,
        order_table.reshape(2, 1, M),
        wigner.reshape(2, L // 2, NBETA, P, SL),
    )


def solution(mesh):
    fits = mesh.shape["order"] == 4 and mesh.shape["degree"] == 2 and mesh.shape["site"] == 4
    shards = fused_shards if fits else general_shards
    in_specs = (
        P(None, None, "degree", "order", None),
        P("site"),
        P(None, None, "degree", "order"),
        P(),
        P("degree", None, "order", None),
    )
    out_specs = P("site", "degree", "order", None)
    return jax.shard_map(shards, mesh=mesh, in_specs=in_specs, out_specs=out_specs, check_vma=False)
```

```python
import math

import jax
import jax.numpy as jnp
from jax import lax
from jax.experimental import pallas as pl
from jax.experimental.pallas import tpu as pltpu
from jax.sharding import PartitionSpec as P


def general_shards(scene_coeffs, site_ids, gripper_coeffs, order_table, wigner):
    highest = lax.Precision.HIGHEST
    slot_count = order_table.shape[0]
    local_deg = gripper_coeffs.shape[2]
    local_ord = gripper_coeffs.shape[3]
    cand_count = scene_coeffs.shape[4]
    site_count = site_ids.shape[0]
    order_pos = lax.axis_index("order")
    degree_pos = lax.axis_index("degree")
    orders = order_table - slot_count // 2
    angles = jnp.arange(slot_count, dtype=jnp.int32)
    phase_index = jnp.mod(orders[:, None] * angles[None, :], slot_count)
    radians = phase_index.astype(jnp.float32) * (2.0 * math.pi / slot_count)
    cosine = jnp.cos(radians)
    sine_table = jnp.sin(radians)
    magnitude = jnp.abs(orders)
    resident_degrees = degree_pos * local_deg + jnp.arange(local_deg, dtype=jnp.int32)
    owned_orders = lax.dynamic_slice_in_dim(magnitude, order_pos * local_ord, local_ord)
    grip_allowed = owned_orders[None, :] <= resident_degrees[:, None]
    selector = (jnp.arange(cand_count, dtype=jnp.int32)[:, None] == site_ids[None, :]).astype(
        jnp.bfloat16
    )
    chosen = jnp.dot(
        scene_coeffs.reshape(-1, cand_count), selector, preferred_element_type=jnp.float32
    )
    chosen = chosen.astype(jnp.bfloat16).reshape(
        2, scene_coeffs.shape[1], local_deg, local_ord, site_count
    )
    grip_real = jnp.concatenate([gripper_coeffs[0], gripper_coeffs[1]], axis=0)
    grip_imag = jnp.concatenate([-gripper_coeffs[1], gripper_coeffs[0]], axis=0)
    gripper_couple = jnp.stack([grip_real, grip_imag])
    columns_in = lax.all_gather(chosen, "order", axis=3, tiled=True)
    scene_joined = jnp.concatenate([columns_in[0], columns_in[1]], axis=0)
    product = jnp.einsum(
        "aonw,iaob->iobnw", scene_joined, gripper_couple, preferred_element_type=jnp.float32
    )
    permitted_mask = grip_allowed[:, :, None] & (
        magnitude[None, None, :] <= resident_degrees[:, None, None]
    )
    product = jnp.where(permitted_mask[None, :, :, :, None], product, jnp.float32(0.0)).astype(
        jnp.bfloat16
    )
    partial_value = jnp.einsum(
        "ylprs,lbpr->ysbpr", product, wigner, preferred_element_type=jnp.float32
    )
    summed = lax.psum_scatter(partial_value, "degree", scatter_dimension=2, tiled=True)
    phase_pair = jnp.concatenate([cosine, sine_table], axis=1)
    products = jnp.einsum(
        "xsbpm,mk->xsbpk", summed, phase_pair, precision=highest, preferred_element_type=jnp.float32
    )
    real_alpha = products[0, ..., :slot_count] - products[1, ..., slot_count:]
    imag_alpha = products[0, ..., slot_count:] + products[1, ..., :slot_count]
    stacked_parts = jnp.stack([real_alpha, imag_alpha])
    exchanged = lax.all_to_all(stacked_parts, "order", split_axis=4, concat_axis=3, tiled=True)
    first_term = jnp.einsum(
        "sbpa,pk->sbak", exchanged[0], cosine, precision=highest, preferred_element_type=jnp.float32
    )
    latter_addend = jnp.einsum(
        "sbpa,pk->sbak",
        exchanged[1],
        sine_table,
        precision=highest,
        preferred_element_type=jnp.float32,
    )
    return first_term - latter_addend


MESH = pl.DeviceIdType.MESH
F32, BF16 = jnp.float32, jnp.bfloat16
CHUNKS = 4
ROWS = 16
GROUP = 8


def cos_of(index, count):
    centred = jnp.bitwise_and(index + count // 2, count - 1) - count // 2
    half = centred.astype(F32) * F32(math.pi / count)
    sq = half * half
    poly = F32(-1.0 / 39916800.0)
    for coefficient in (1.0 / 362880.0, -1.0 / 5040.0, 1.0 / 120.0, -1.0 / 6.0, 1.0):
        poly = poly * sq + F32(coefficient)
    sine = poly * half
    return 1.0 - 2.0 * sine * sine


def split(value):
    high = value.astype(BF16)
    return high, (value - high.astype(F32)).astype(BF16)


def fused_kernel(
    scene_ref, site_ref, g_hbm, row_hbm, w_ref, out_ref, wbuf, *scratch
):
    cands, scratch = scratch[:CHUNKS], scratch[CHUNKS:]
    fused_body(scene_ref, site_ref, g_hbm, row_hbm, w_ref, out_ref, wbuf, cands, *scratch)


def fused_body(
    scene_ref, site_ref, g_hbm, row_hbm, w_ref, out_ref, wbuf, cands,
    g_ref, row_ref, sbuf, prod, accbuf, rs_send, rs_recv, a_send, a_recv, halfacc,
    alpha_hi, alpha_lo, gamma_hi, gamma_lo, g32, col,
    in_sem, c_sem, w_sem, s_send_sem, s_recv_sem, r_send_sem, r_recv_sem, x_send_sem, x_recv_sem,
):
    me = lax.axis_index("order")
    deg = lax.axis_index("degree")
    HL, NBETA, P, M = wbuf.shape[2:]
    L = 2 * HL
    SL = 2 * M
    BO = NBETA // 2
    K = scene_ref.shape[0]
    first = me // 2
    second = 1 - first
    near = first * 2 + (1 - me % 2)
    per = HL // CHUNKS
    blocks = P // ROWS

    def w_copy(h, c):
        return pltpu.make_async_copy(
            w_ref.at[:, pl.ds(c * per, per), :, :, pl.ds(pl.multiple_of(h * M, M), M)],
            wbuf.at[h, :, pl.ds(c * per, per)],
            w_sem.at[h, c],
        )

    def c_copy(c):
        return pltpu.make_async_copy(
            scene_ref.at[:, :, pl.ds(c * per, per)], cands[c], c_sem.at[c]
        )

    c_copy(0).start()
    g_copy = pltpu.make_async_copy(g_hbm, g_ref, in_sem.at[0])
    row_copy = pltpu.make_async_copy(row_hbm, row_ref, in_sem.at[1])
    row_copy.start()
    g_copy.start()
    for c in range(1, CHUNKS):
        c_copy(c).start()

    barrier = pltpu.get_barrier_semaphore()
    for off in (1, 2, 3):
        pl.semaphore_signal(barrier, 1, device_id={"order": (me + off) % 4}, device_id_type=MESH)
    pl.semaphore_signal(barrier, 1, device_id={"degree": 1 - deg}, device_id_type=MESH)

    site = site_ref[0]
    pick_row = lax.broadcasted_iota(jnp.int32, (K, K * GROUP), 0)
    pick_col = lax.broadcasted_iota(jnp.int32, (K, K * GROUP), 1)
    pick = (pick_col == pick_row * GROUP + site % GROUP).astype(F32).astype(BF16)

    def select(c):
        def step(i, carry):
            halves = []
            for part in range(2):
                tile = cands[c][:, part, i, site // GROUP].astype(F32)
                tile = tile.reshape(K * GROUP, P).astype(BF16)
                halves.append(jnp.dot(pick, tile, preferred_element_type=F32))
            sbuf[me, c * per + i] = jnp.concatenate(halves, axis=1).astype(BF16)
            return carry

        c_copy(c).wait()
        lax.fori_loop(0, per, step, 0, unroll=True)

    def hop(block, c, way):
        rows = pl.ds(c * per, per)
        return pltpu.make_async_remote_copy(
            src_ref=sbuf.at[block, rows],
            dst_ref=sbuf.at[block, rows],
            send_sem=s_send_sem.at[way, block, c], recv_sem=s_recv_sem.at[block, c],
            device_id={"order": me + 1 - 2 * way}, device_id_type=MESH,
        )

    def send_own(c):
        @pl.when(me < 3)
        def _():
            hop(me, c, 0).start()

        @pl.when(me > 0)
        def _():
            hop(me, c, 1).start()

    def prepare():
        row_copy.wait()
        for h in range(2):
            line = jnp.broadcast_to(row_ref[h].astype(F32), (M, M))
            col[h * M : (h + 1) * M, :] = jnp.transpose(line).astype(jnp.int32) - SL // 2
        g_copy.wait()
        real = g_ref[0].astype(F32).reshape(K // 2 * L, P)
        imag = g_ref[1].astype(F32).reshape(K // 2 * L, P)
        g32[: K // 2 * L] = jnp.concatenate([real, -imag], axis=1)
        g32[K // 2 * L :] = jnp.concatenate([imag, real], axis=1)
        accbuf[...] = jnp.zeros_like(accbuf)

    dims = (((0,), (0,)), ((), ()))

    def tables():
        quarter = SL // 4
        lane = lax.broadcasted_iota(jnp.int32, (M, M), 1)
        for h in range(2):
            orders = col[h * M : (h + 1) * M, :]
            for t in range(4):
                at = slice(t * M, (t + 1) * M)
                phase = orders * (t * P + lane % P)
                for x in range(2):
                    hi, lo = split(cos_of(phase + (x - lane // P) * quarter, SL))
                    alpha_hi[h, x * M : (x + 1) * M, at] = hi
                    alpha_lo[h, x * M : (x + 1) * M, at] = lo
                phase = orders * ((t % 2) * M + lane)
                hi, lo = split(cos_of(phase + (t // 2) * quarter, SL))
                gamma_hi[h * M : (h + 1) * M, at] = hi
                gamma_lo[h * M : (h + 1) * M, at] = lo

    def r_copy(h, blk):
        return pltpu.make_async_remote_copy(
            src_ref=rs_send.at[h, blk], dst_ref=rs_recv.at[h, blk],
            send_sem=r_send_sem.at[h, blk], recv_sem=r_recv_sem.at[h, blk],
            device_id={"degree": 1 - deg}, device_id_type=MESH,
        )

    def compute(h, before, after):
        mag_p = jnp.abs(col[pl.ds(pl.multiple_of(me * P, P), P), :])
        mag_m = jnp.abs(row_ref[h] - SL // 2)
        most = jnp.maximum(mag_p, jnp.broadcast_to(mag_m, (P, M)))
        most = jnp.concatenate([most, most], axis=0)

        def chunk(c, carry):
            before(c)
            for i in range(per):
                step = c * per + i
                b0, b1 = sbuf[2 * h, step], sbuf[2 * h + 1, step]
                low = jnp.concatenate([b0[:, :P], b1[:, :P]], axis=1)
                high = jnp.concatenate([b0[:, P:], b1[:, P:]], axis=1)
                for part, scene in ((0, low), (1, high)):
                    l = step + part * HL
                    grip = g32[pl.ds(l, K, stride=L), :].astype(BF16)
                    value = lax.dot_general(grip, scene, dims, preferred_element_type=F32)
                    value = jnp.where(most <= deg * L + l, value, F32(0.0))
                    prod[part, i] = value.astype(BF16)
            w_copy(h, c).wait()

            def rows(blk, carry):
                at = pl.multiple_of(blk * ROWS, ROWS)

                def degree_step(i, acc):
                    acc = list(acc)
                    for part in range(2):
                        pr = prod[part, i, pl.ds(at, ROWS), :].astype(F32)
                        pi = prod[part, i, pl.ds(at + P, ROWS), :].astype(F32)
                        for b in range(NBETA):
                            w = wbuf[h, part, c * per + i, b, pl.ds(at, ROWS), :].astype(F32)
                            acc[2 * b] += pr * w
                            acc[2 * b + 1] += pi * w
                    return tuple(acc)

                acc = tuple(accbuf[h, blk, n // 2, n % 2] for n in range(2 * NBETA))
                acc = lax.fori_loop(0, per, degree_step, acc, unroll=2)
                for n in range(2 * NBETA):
                    accbuf[h, blk, n // 2, n % 2] = acc[n]

                @pl.when(c == CHUNKS - 1)
                def _():
                    rs_send[h, blk] = accbuf[h, blk, pl.ds((1 - deg) * BO, BO)].astype(BF16)
                    r_copy(h, blk).start()

                return carry

            lax.fori_loop(0, blocks, rows, 0)
            after(c)
            return carry

        lax.fori_loop(0, CHUNKS, chunk, 0)

    def alpha(h, blk):
        r_copy(h, blk).wait_recv()
        total = accbuf[h, blk, pl.ds(deg * BO, BO)] + rs_recv[h, blk].astype(F32)
        total = jnp.concatenate(
            [total[:, 0].reshape(BO * ROWS, M), total[:, 1].reshape(BO * ROWS, M)], axis=1
        )
        hi, lo = split(total)
        value = jnp.dot(hi, alpha_hi[h], preferred_element_type=F32)
        value += jnp.dot(hi, alpha_lo[h], preferred_element_type=F32)
        value += jnp.dot(lo, alpha_hi[h], preferred_element_type=F32)
        return value

    across = lax.max(me - 1, 0) % 2
    middle = (me == 1) | (me == 2)
    other = me + 1 - 2 * across
    beyond = other + 1 - 2 * across

    def wait_block(block, c):
        hop(block, c, me // 3).wait_recv()

    def collect(c):
        wait_block(near, c)

        @pl.when(middle)
        def _():
            hop(near, c, across).start()
            wait_block(other, c)
            hop(other, c, 1 - across).start()

    def relay(c):
        @pl.when(middle)
        def _():
            wait_block(beyond, c)
            hop(beyond, c, 1 - across).start()

    def after_first(c):
        @pl.when(c < CHUNKS - 2)
        def _():
            collect(c + 2)

        @pl.when(c > 0)
        def _():
            relay(c - 1)

    def before_second(c):
        @pl.when(jnp.logical_not(middle))
        def _():
            wait_block(second * 2, c)
            wait_block(second * 2 + 1, c)

        @pl.when(c == 2)
        def _():
            for blk in range(blocks):
                halfacc[blk] = alpha(first, blk)

    select(0)
    pl.semaphore_wait(barrier, 4)
    send_own(0)
    select(1)
    send_own(1)
    w_copy(first, 0).start()
    select(2)
    send_own(2)
    w_copy(first, 1).start()
    collect(0)
    select(3)
    send_own(3)
    for c in range(2, CHUNKS):
        w_copy(first, c).start()
    for c in range(CHUNKS):
        w_copy(second, c).start()
    collect(1)
    prepare()
    compute(first, lambda c: None, after_first)
    tables()
    relay(CHUNKS - 1)
    compute(second, before_second, lambda c: None)

    def x_copy(target, source, blk, off):
        return pltpu.make_async_remote_copy(
            src_ref=a_send.at[target, blk], dst_ref=a_recv.at[source, blk],
            send_sem=x_send_sem.at[off, blk], recv_sem=x_recv_sem.at[off, blk],
            device_id={"order": target}, device_id_type=MESH,
        )

    for blk in range(blocks):
        value = (halfacc[blk] + alpha(second, blk)).astype(BF16)
        for t in range(4):
            a_send[t, blk] = value[:, t * M : (t + 1) * M]
        for off in (2, 1, 3):
            x_copy((me + off) % 4, me, blk, off).start()
        a_recv[me, blk] = a_send[me, blk]

    for blk in range(blocks):
        for off in (1, 3, 2):
            source = (me - off + 4) % 4
            x_copy(source, source, blk, off).wait_recv()

    score = jnp.zeros((BO * P, SL), F32)
    got = [
        jnp.concatenate(
            [a_recv[z, blk, b * ROWS : (b + 1) * ROWS, :] for z in range(4) for blk in range(blocks)],
            axis=0,
        )
        for b in range(BO)
    ]
    for x in range(2):
        left = jnp.concatenate([piece[:, x * P : (x + 1) * P] for piece in got], axis=1)
        for table in (gamma_hi, gamma_lo):
            score += lax.dot_general(
                left, table[:, x * SL : (x + 1) * SL], dims, preferred_element_type=F32
            )
    out_ref[0] = score.reshape(BO, P, SL)

    for c in range(CHUNKS):
        @pl.when(me < 3)
        def _():
            hop(me, c, 0).wait_send()

        @pl.when(me > 0)
        def _():
            hop(me, c, 1).wait_send()

        @pl.when(middle)
        def _():
            hop(near, c, across).wait_send()
            hop(other, c, 1 - across).wait_send()
            hop(beyond, c, 1 - across).wait_send()

    for blk in range(blocks):
        for off in (1, 2, 3):
            x_copy((me + off) % 4, me, blk, off).wait_send()
        r_copy(first, blk).wait_send()
        r_copy(second, blk).wait_send()


def fused_shards(scene_coeffs, site_ids, gripper_coeffs, order_table, wigner):
    L, NBETA, P, SL = wigner.shape
    M = SL // 2
    K = 2 * scene_coeffs.shape[1]
    BO = NBETA // 2
    NB = P // ROWS
    cand = scene_coeffs.shape[4]
    tall = jnp.transpose(scene_coeffs, (0, 1, 2, 4, 3))
    tall = tall.reshape(K, 2, L // 2, cand // GROUP, GROUP, P)
    vmem = pl.BlockSpec(memory_space=pltpu.VMEM)
    hbm = pl.BlockSpec(memory_space=pltpu.HBM)
    return pl.pallas_call(
        fused_kernel,
        out_shape=jax.ShapeDtypeStruct((1, BO, P, SL), F32),
        in_specs=[hbm, pl.BlockSpec(memory_space=pltpu.SMEM), hbm, hbm, hbm],
        out_specs=vmem,
        scratch_shapes=[
            pltpu.VMEM((2, 2, L // 2, NBETA, P, M), BF16),
            *[
                pltpu.VMEM((K, 2, L // 2 // CHUNKS, cand // GROUP, GROUP, P), BF16)
                for _ in range(CHUNKS)
            ],
            pltpu.VMEM((2, K // 2, L, P), BF16),
            pltpu.VMEM((2, 1, M), jnp.int32),
            pltpu.VMEM((4, L // 2, K, 2 * P), BF16),
            pltpu.VMEM((2, L // 2 // CHUNKS, 2 * P, M), BF16),
            pltpu.VMEM((2, NB, NBETA, 2, ROWS, M), F32),
            pltpu.VMEM((2, NB, BO, 2, ROWS, M), BF16),
            pltpu.VMEM((2, NB, BO, 2, ROWS, M), BF16),
            pltpu.VMEM((4, NB, BO * ROWS, M), BF16),
            pltpu.VMEM((4, NB, BO * ROWS, M), BF16),
            pltpu.VMEM((NB, BO * ROWS, 2 * SL), F32),
            pltpu.VMEM((2, 2 * M, 2 * SL), BF16),
            pltpu.VMEM((2, 2 * M, 2 * SL), BF16),
            pltpu.VMEM((SL, 2 * SL), BF16),
            pltpu.VMEM((SL, 2 * SL), BF16),
            pltpu.VMEM((K * L, 2 * P), F32),
            pltpu.VMEM((SL, M), jnp.int32),
            pltpu.SemaphoreType.DMA((2,)),
            pltpu.SemaphoreType.DMA((CHUNKS,)),
            pltpu.SemaphoreType.DMA((2, CHUNKS)),
            pltpu.SemaphoreType.DMA((2, 4, CHUNKS)),
            pltpu.SemaphoreType.DMA((4, CHUNKS)),
            pltpu.SemaphoreType.DMA((2, NB)),
            pltpu.SemaphoreType.DMA((2, NB)),
            pltpu.SemaphoreType.DMA((4, NB)),
            pltpu.SemaphoreType.DMA((4, NB)),
        ],
        compiler_params=pltpu.CompilerParams(
            collective_id=0, has_side_effects=True, vmem_limit_bytes=48 * 1024 * 1024
        ),
    )(
        tall,
        site_ids,
        pltpu.with_memory_space_constraint(gripper_coeffs, pltpu.HBM),
        pltpu.with_memory_space_constraint(order_table.reshape(2, 1, M), pltpu.HBM),
        wigner.reshape(2, L // 2, NBETA, P, SL),
    )


def solution(mesh):
    fits = mesh.shape["order"] == 4 and mesh.shape["degree"] == 2 and mesh.shape["site"] == 4
    shards = fused_shards if fits else general_shards
    in_specs = (
        P(None, None, "degree", "order", None),
        P("site"),
        P(None, None, "degree", "order"),
        P(),
        P("degree", None, "order", None),
    )
    out_specs = P("site", "degree", "order", None)
    return jax.shard_map(shards, mesh=mesh, in_specs=in_specs, out_specs=out_specs, check_vma=False)
```

```python
import math

import jax
import jax.numpy as jnp
from jax import lax
from jax.experimental import pallas as pl
from jax.experimental.pallas import tpu as pltpu
from jax.sharding import PartitionSpec as P


def general_shards(scene_coeffs, site_ids, gripper_coeffs, order_table, wigner):
    highest = lax.Precision.HIGHEST
    slot_count = order_table.shape[0]
    local_deg = gripper_coeffs.shape[2]
    local_ord = gripper_coeffs.shape[3]
    cand_count = scene_coeffs.shape[4]
    site_count = site_ids.shape[0]
    order_pos = lax.axis_index("order")
    degree_pos = lax.axis_index("degree")
    orders = order_table - slot_count // 2
    angles = jnp.arange(slot_count, dtype=jnp.int32)
    phase_index = jnp.mod(orders[:, None] * angles[None, :], slot_count)
    radians = phase_index.astype(jnp.float32) * (2.0 * math.pi / slot_count)
    cosine = jnp.cos(radians)
    sine_table = jnp.sin(radians)
    magnitude = jnp.abs(orders)
    resident_degrees = degree_pos * local_deg + jnp.arange(local_deg, dtype=jnp.int32)
    owned_orders = lax.dynamic_slice_in_dim(magnitude, order_pos * local_ord, local_ord)
    grip_allowed = owned_orders[None, :] <= resident_degrees[:, None]
    selector = (jnp.arange(cand_count, dtype=jnp.int32)[:, None] == site_ids[None, :]).astype(
        jnp.bfloat16
    )
    chosen = jnp.dot(
        scene_coeffs.reshape(-1, cand_count), selector, preferred_element_type=jnp.float32
    )
    chosen = chosen.astype(jnp.bfloat16).reshape(
        2, scene_coeffs.shape[1], local_deg, local_ord, site_count
    )
    grip_real = jnp.concatenate([gripper_coeffs[0], gripper_coeffs[1]], axis=0)
    grip_imag = jnp.concatenate([-gripper_coeffs[1], gripper_coeffs[0]], axis=0)
    gripper_couple = jnp.stack([grip_real, grip_imag])
    columns_in = lax.all_gather(chosen, "order", axis=3, tiled=True)
    scene_joined = jnp.concatenate([columns_in[0], columns_in[1]], axis=0)
    product = jnp.einsum(
        "aonw,iaob->iobnw", scene_joined, gripper_couple, preferred_element_type=jnp.float32
    )
    permitted_mask = grip_allowed[:, :, None] & (
        magnitude[None, None, :] <= resident_degrees[:, None, None]
    )
    product = jnp.where(permitted_mask[None, :, :, :, None], product, jnp.float32(0.0)).astype(
        jnp.bfloat16
    )
    partial_value = jnp.einsum(
        "ylprs,lbpr->ysbpr", product, wigner, preferred_element_type=jnp.float32
    )
    summed = lax.psum_scatter(partial_value, "degree", scatter_dimension=2, tiled=True)
    phase_pair = jnp.concatenate([cosine, sine_table], axis=1)
    products = jnp.einsum(
        "xsbpm,mk->xsbpk", summed, phase_pair, precision=highest, preferred_element_type=jnp.float32
    )
    real_alpha = products[0, ..., :slot_count] - products[1, ..., slot_count:]
    imag_alpha = products[0, ..., slot_count:] + products[1, ..., :slot_count]
    stacked_parts = jnp.stack([real_alpha, imag_alpha])
    exchanged = lax.all_to_all(stacked_parts, "order", split_axis=4, concat_axis=3, tiled=True)
    first_term = jnp.einsum(
        "sbpa,pk->sbak", exchanged[0], cosine, precision=highest, preferred_element_type=jnp.float32
    )
    latter_addend = jnp.einsum(
        "sbpa,pk->sbak",
        exchanged[1],
        sine_table,
        precision=highest,
        preferred_element_type=jnp.float32,
    )
    return first_term - latter_addend


MESH = pl.DeviceIdType.MESH
F32, BF16 = jnp.float32, jnp.bfloat16
CHUNKS = 4
PIECES = (8, 8, 8, 8)
STAGED = 4
PLAN = (
    "s0 s1 s2 s3",
    "f0 f1 f2 f3",
    "x c0 p c1",
    "u0 c2 u1 c3",
    "r0 u2 r1 u3",
    "r2 t r3 v0",
    "v1 v2 v3 a",
)
UNITS = ((0, 8, (0,)), (8, 8, (1,)), (16, 8, (2,)), (24, 8, (3,)))
ROWS = 16
GROUP = 8


def cos_of(index, count):
    centred = jnp.bitwise_and(index + count // 2, count - 1) - count // 2
    half = centred.astype(F32) * F32(math.pi / count)
    sq = half * half
    poly = F32(-1.0 / 39916800.0)
    for coefficient in (1.0 / 362880.0, -1.0 / 5040.0, 1.0 / 120.0, -1.0 / 6.0, 1.0):
        poly = poly * sq + F32(coefficient)
    sine = poly * half
    return 1.0 - 2.0 * sine * sine


def split(value):
    high = value.astype(BF16)
    return high, (value - high.astype(F32)).astype(BF16)


def fused_kernel(
    scene_ref, site_ref, g_hbm, row_hbm, w_ref, out_ref, wbuf, *scratch
):
    cands, scratch = scratch[: len(PIECES)], scratch[len(PIECES) :]
    fused_body(scene_ref, site_ref, g_hbm, row_hbm, w_ref, out_ref, wbuf, cands, *scratch)


def fused_body(
    scene_ref, site_ref, g_hbm, row_hbm, w_ref, out_ref, wbuf, cands,
    g_ref, row_ref, sbuf, prod, accbuf, rs_send, rs_recv, a_send, a_recv, halfacc,
    alpha_hi, alpha_lo, gamma_hi, gamma_lo, g32, col,
    in_sem, c_sem, w_sem, s_send_sem, s_recv_sem, r_send_sem, r_recv_sem, x_send_sem, x_recv_sem,
):
    me = lax.axis_index("order")
    deg = lax.axis_index("degree")
    HL, NBETA, P, M = wbuf.shape[2:]
    L = 2 * HL
    SL = 2 * M
    BO = NBETA // 2
    K = scene_ref.shape[0]
    first = me // 2
    second = 1 - first
    near = first * 2 + (1 - me % 2)
    per = HL // CHUNKS
    blocks = P // ROWS

    def w_copy(h, c):
        return pltpu.make_async_copy(
            w_ref.at[:, pl.ds(c * per, per), :, :, pl.ds(pl.multiple_of(h * M, M), M)],
            wbuf.at[h, :, pl.ds(c * per, per)],
            w_sem.at[h, c],
        )

    starts = [sum(PIECES[:i]) for i in range(len(PIECES))]

    def c_copy(c):
        return pltpu.make_async_copy(
            scene_ref.at[:, :, pl.ds(starts[c], PIECES[c])], cands[c], c_sem.at[c]
        )

    c_copy(0).start()
    g_copy = pltpu.make_async_copy(g_hbm, g_ref, in_sem.at[0])
    row_copy = pltpu.make_async_copy(row_hbm, row_ref, in_sem.at[1])
    row_copy.start()
    g_copy.start()
    for c in range(1, STAGED):
        c_copy(c).start()

    barrier = pltpu.get_barrier_semaphore()
    for off in (1, 2, 3):
        pl.semaphore_signal(barrier, 1, device_id={"order": (me + off) % 4}, device_id_type=MESH)
    pl.semaphore_signal(barrier, 1, device_id={"degree": 1 - deg}, device_id_type=MESH)

    site = site_ref[0]
    pick_row = lax.broadcasted_iota(jnp.int32, (K, K * GROUP), 0)
    pick_col = lax.broadcasted_iota(jnp.int32, (K, K * GROUP), 1)
    pick = (pick_col == pick_row * GROUP + site % GROUP).astype(F32).astype(BF16)

    def select(c):
        def step(i, carry):
            halves = []
            for part in range(2):
                tile = cands[c][:, part, i, site // GROUP].reshape(K * GROUP, P)
                halves.append(jnp.dot(pick, tile, preferred_element_type=F32))
            sbuf[me, starts[c] + i] = jnp.concatenate(halves, axis=1).astype(BF16)
            return carry

        c_copy(c).wait()
        lax.fori_loop(0, PIECES[c], step, 0, unroll=True)

    def hop(block, c, way):
        rows = pl.ds(starts[c], PIECES[c])
        return pltpu.make_async_remote_copy(
            src_ref=sbuf.at[block, rows],
            dst_ref=sbuf.at[block, rows],
            send_sem=s_send_sem.at[way, block, c], recv_sem=s_recv_sem.at[block, c],
            device_id={"order": me + 1 - 2 * way}, device_id_type=MESH,
        )

    def send_own(c):
        @pl.when(me < 3)
        def _():
            hop(me, c, 0).start()

        @pl.when(me > 0)
        def _():
            hop(me, c, 1).start()

    def prepare():
        row_copy.wait()
        for h in range(2):
            line = jnp.broadcast_to(row_ref[h].astype(F32), (M, M))
            col[h * M : (h + 1) * M, :] = jnp.transpose(line).astype(jnp.int32) - SL // 2
        g_copy.wait()
        real = g_ref[0].astype(F32).reshape(K // 2 * L, P)
        imag = g_ref[1].astype(F32).reshape(K // 2 * L, P)
        g32[: K // 2 * L] = jnp.concatenate([real, -imag], axis=1)
        g32[K // 2 * L :] = jnp.concatenate([imag, real], axis=1)
        accbuf[...] = jnp.zeros_like(accbuf)

    dims = (((0,), (0,)), ((), ()))

    def tables():
        quarter = SL // 4
        lane = lax.broadcasted_iota(jnp.int32, (M, M), 1)
        left = lane < P
        for h in range(2):
            orders = col[h * M : (h + 1) * M, :]
            upright, turned = [], []
            for t in range(4):
                at = slice(t * M, (t + 1) * M)
                phase = orders * (t * P + lane % P) - (lane // P) * quarter
                upright.append(cos_of(phase, SL))
                swapped = pltpu.roll(upright[t], P, 1)
                turned.append(jnp.where(left, -swapped, swapped))
                for x, value in ((0, upright[t]), (1, turned[t])):
                    hi, lo = split(value)
                    alpha_hi[h, x * M : (x + 1) * M, at] = hi
                    alpha_lo[h, x * M : (x + 1) * M, at] = lo
            for t in range(4):
                at = slice(t * M, (t + 1) * M)
                one = t % 2 * 2
                if t < 2:
                    value = jnp.where(left, upright[one], turned[one + 1])
                else:
                    value = jnp.where(left, turned[one], -upright[one + 1])
                hi, lo = split(value)
                gamma_hi[h * M : (h + 1) * M, at] = hi
                gamma_lo[h * M : (h + 1) * M, at] = lo

    def r_copy(h, blk):
        return pltpu.make_async_remote_copy(
            src_ref=rs_send.at[h, blk], dst_ref=rs_recv.at[h, blk],
            send_sem=r_send_sem.at[h, blk], recv_sem=r_recv_sem.at[h, blk],
            device_id={"degree": 1 - deg}, device_id_type=MESH,
        )

    def unit(h, start, size, last):
        mag_p = jnp.abs(col[pl.ds(pl.multiple_of(me * P, P), P), :])
        mag_m = jnp.abs(row_ref[h] - SL // 2)
        most = jnp.maximum(mag_p, jnp.broadcast_to(mag_m, (P, M)))
        most = jnp.concatenate([most, most], axis=0)
        for i in range(size):
            step = start + i
            b0, b1 = sbuf[2 * h, step], sbuf[2 * h + 1, step]
            low = jnp.concatenate([b0[:, :P], b1[:, :P]], axis=1)
            high = jnp.concatenate([b0[:, P:], b1[:, P:]], axis=1)
            for part, scene in ((0, low), (1, high)):
                l = step + part * HL
                grip = g32[pl.ds(l, K, stride=L), :].astype(BF16)
                value = lax.dot_general(grip, scene, dims, preferred_element_type=F32)
                value = jnp.where(most <= deg * L + l, value, F32(0.0))
                prod[part, i] = value.astype(BF16)

        def rows(blk, carry):
            at = pl.multiple_of(blk * ROWS, ROWS)

            def degree_step(i, acc):
                acc = list(acc)
                for part in range(2):
                    pr = prod[part, i, pl.ds(at, ROWS), :].astype(F32)
                    pi = prod[part, i, pl.ds(at + P, ROWS), :].astype(F32)
                    for b in range(NBETA):
                        w = wbuf[h, part, start + i, b, pl.ds(at, ROWS), :].astype(F32)
                        acc[2 * b] += pr * w
                        acc[2 * b + 1] += pi * w
                return tuple(acc)

            acc = tuple(accbuf[h, blk, n // 2, n % 2] for n in range(2 * NBETA))
            acc = lax.fori_loop(0, size, degree_step, acc, unroll=2)
            for n in range(2 * NBETA):
                accbuf[h, blk, n // 2, n % 2] = acc[n]

            def scatter():
                rs_send[h, blk] = accbuf[h, blk, pl.ds((1 - deg) * BO, BO)].astype(BF16)
                r_copy(h, blk).start()

            if isinstance(last, bool):
                if last:
                    scatter()
            else:
                pl.when(last)(scatter)

            return carry

        lax.fori_loop(0, blocks, rows, 0)

    def alpha(h, blk):
        r_copy(h, blk).wait_recv()
        total = accbuf[h, blk, pl.ds(deg * BO, BO)] + rs_recv[h, blk].astype(F32)
        total = jnp.concatenate(
            [total[:, 0].reshape(BO * ROWS, M), total[:, 1].reshape(BO * ROWS, M)], axis=1
        )
        hi, lo = split(total)
        value = jnp.dot(hi, alpha_hi[h], preferred_element_type=F32)
        value += jnp.dot(hi, alpha_lo[h], preferred_element_type=F32)
        value += jnp.dot(lo, alpha_hi[h], preferred_element_type=F32)
        return value

    across = lax.max(me - 1, 0) % 2
    middle = (me == 1) | (me == 2)
    other = me + 1 - 2 * across
    beyond = other + 1 - 2 * across

    def wait_block(block, c):
        hop(block, c, me // 3).wait_recv()

    def collect(c):
        wait_block(near, c)

        @pl.when(middle)
        def _():
            hop(near, c, across).start()
            wait_block(other, c)
            hop(other, c, 1 - across).start()

    def relay(c):
        @pl.when(middle)
        def _():
            wait_block(beyond, c)
            hop(beyond, c, 1 - across).start()

    def wait_second(i):
        @pl.when(jnp.logical_not(middle))
        def _():
            wait_block(second * 2, i)
            wait_block(second * 2 + 1, i)

    def own(i):
        select(i)
        if i == 0:
            pl.semaphore_wait(barrier, 4)
        send_own(i)

    def fetch_first(c):
        w_copy(first, c).start()

    def fetch_second():
        for c in range(CHUNKS):
            w_copy(second, c).start()

    def unit_first(c):
        w_copy(first, c).wait()
        unit(first, c * per, per, c == CHUNKS - 1)

    def unit_second(n):
        start, size, pieces = UNITS[n]
        for i in pieces:
            wait_second(i)
        if start % per == 0:
            w_copy(second, start // per).wait()
        unit(second, start, size, n == len(UNITS) - 1)

    def alpha_first():
        for blk in range(blocks):
            halfacc[blk] = alpha(first, blk)

    def stage(c):
        c_copy(c).start()

    acts = {
        "s": own, "c": collect, "r": relay, "f": fetch_first, "x": fetch_second, "p": prepare,
        "t": tables, "u": unit_first, "v": unit_second, "a": alpha_first, "k": stage,
    }
    for item in sum((part.split() for part in PLAN), []):
        acts[item[0]](*[int(item[1:])] if item[1:] else [])

    def x_copy(target, source, blk, off):
        return pltpu.make_async_remote_copy(
            src_ref=a_send.at[target, blk], dst_ref=a_recv.at[source, blk],
            send_sem=x_send_sem.at[off, blk], recv_sem=x_recv_sem.at[off, blk],
            device_id={"order": target}, device_id_type=MESH,
        )

    for blk in range(blocks):
        value = (halfacc[blk] + alpha(second, blk)).astype(BF16)
        for t in range(4):
            a_send[t, blk] = value[:, t * M : (t + 1) * M]
        for off in (3, 2, 1):
            far = jnp.where(me < 2, (me + off) % 4, (me - off + 4) % 4)
            x_copy(far, me, blk, (far - me + 4) % 4).start()
        a_recv[me, blk] = a_send[me, blk]

    for blk in range(blocks):
        for off in (1, 3, 2):
            source = (me - off + 4) % 4
            x_copy(source, source, blk, off).wait_recv()

    score = jnp.zeros((BO * P, SL), F32)
    got = [
        jnp.concatenate(
            [a_recv[z, blk, b * ROWS : (b + 1) * ROWS, :] for z in range(4) for blk in range(blocks)],
            axis=0,
        )
        for b in range(BO)
    ]
    for x in range(2):
        left = jnp.concatenate([piece[:, x * P : (x + 1) * P] for piece in got], axis=1)
        for table in (gamma_hi, gamma_lo):
            score += lax.dot_general(
                left, table[:, x * SL : (x + 1) * SL], dims, preferred_element_type=F32
            )
    out_ref[0] = score.reshape(BO, P, SL)

    for c in range(len(PIECES)):
        @pl.when(me < 3)
        def _():
            hop(me, c, 0).wait_send()

        @pl.when(me > 0)
        def _():
            hop(me, c, 1).wait_send()

        @pl.when(middle)
        def _():
            hop(near, c, across).wait_send()
            hop(other, c, 1 - across).wait_send()
            hop(beyond, c, 1 - across).wait_send()

    for blk in range(blocks):
        for off in (1, 2, 3):
            x_copy((me + off) % 4, me, blk, off).wait_send()
        r_copy(first, blk).wait_send()
        r_copy(second, blk).wait_send()


def fused_shards(scene_coeffs, site_ids, gripper_coeffs, order_table, wigner):
    L, NBETA, P, SL = wigner.shape
    M = SL // 2
    K = 2 * scene_coeffs.shape[1]
    BO = NBETA // 2
    NB = P // ROWS
    cand = scene_coeffs.shape[4]
    tall = jnp.transpose(scene_coeffs, (0, 1, 2, 4, 3))
    tall = tall.reshape(K, 2, L // 2, cand // GROUP, GROUP, P)
    vmem = pl.BlockSpec(memory_space=pltpu.VMEM)
    hbm = pl.BlockSpec(memory_space=pltpu.HBM)
    return pl.pallas_call(
        fused_kernel,
        out_shape=jax.ShapeDtypeStruct((1, BO, P, SL), F32),
        in_specs=[hbm, pl.BlockSpec(memory_space=pltpu.SMEM), hbm, hbm, hbm],
        out_specs=vmem,
        scratch_shapes=[
            pltpu.VMEM((2, 2, L // 2, NBETA, P, M), BF16),
            *[
                pltpu.VMEM((K, 2, size, cand // GROUP, GROUP, P), BF16) for size in PIECES
            ],
            pltpu.VMEM((2, K // 2, L, P), BF16),
            pltpu.VMEM((2, 1, M), jnp.int32),
            pltpu.VMEM((4, L // 2, K, 2 * P), BF16),
            pltpu.VMEM((2, L // 2 // CHUNKS, 2 * P, M), BF16),
            pltpu.VMEM((2, NB, NBETA, 2, ROWS, M), F32),
            pltpu.VMEM((2, NB, BO, 2, ROWS, M), BF16),
            pltpu.VMEM((2, NB, BO, 2, ROWS, M), BF16),
            pltpu.VMEM((4, NB, BO * ROWS, M), BF16),
            pltpu.VMEM((4, NB, BO * ROWS, M), BF16),
            pltpu.VMEM((NB, BO * ROWS, 2 * SL), F32),
            pltpu.VMEM((2, 2 * M, 2 * SL), BF16),
            pltpu.VMEM((2, 2 * M, 2 * SL), BF16),
            pltpu.VMEM((SL, 2 * SL), BF16),
            pltpu.VMEM((SL, 2 * SL), BF16),
            pltpu.VMEM((K * L, 2 * P), F32),
            pltpu.VMEM((SL, M), jnp.int32),
            pltpu.SemaphoreType.DMA((2,)),
            pltpu.SemaphoreType.DMA((len(PIECES),)),
            pltpu.SemaphoreType.DMA((2, CHUNKS)),
            pltpu.SemaphoreType.DMA((2, 4, len(PIECES))),
            pltpu.SemaphoreType.DMA((4, len(PIECES))),
            pltpu.SemaphoreType.DMA((2, NB)),
            pltpu.SemaphoreType.DMA((2, NB)),
            pltpu.SemaphoreType.DMA((4, NB)),
            pltpu.SemaphoreType.DMA((4, NB)),
        ],
        compiler_params=pltpu.CompilerParams(
            collective_id=0, has_side_effects=True, vmem_limit_bytes=48 * 1024 * 1024
        ),
    )(
        tall,
        site_ids,
        pltpu.with_memory_space_constraint(gripper_coeffs, pltpu.HBM),
        pltpu.with_memory_space_constraint(order_table.reshape(2, 1, M), pltpu.HBM),
        wigner.reshape(2, L // 2, NBETA, P, SL),
    )


def solution(mesh):
    fits = mesh.shape["order"] == 4 and mesh.shape["degree"] == 2 and mesh.shape["site"] == 4
    shards = fused_shards if fits else general_shards
    in_specs = (
        P(None, None, "degree", "order", None),
        P("site"),
        P(None, None, "degree", "order"),
        P(),
        P("degree", None, "order", None),
    )
    out_specs = P("site", "degree", "order", None)
    return jax.shard_map(shards, mesh=mesh, in_specs=in_specs, out_specs=out_specs, check_vma=False)
```

```python
import math

import jax
import jax.numpy as jnp
from jax import lax
from jax.experimental import pallas as pl
from jax.experimental.pallas import tpu as pltpu
from jax.sharding import PartitionSpec as P


def general_shards(scene_coeffs, site_ids, gripper_coeffs, order_table, wigner):
    highest = lax.Precision.HIGHEST
    slot_count = order_table.shape[0]
    local_deg = gripper_coeffs.shape[2]
    local_ord = gripper_coeffs.shape[3]
    cand_count = scene_coeffs.shape[4]
    site_count = site_ids.shape[0]
    order_pos = lax.axis_index("order")
    degree_pos = lax.axis_index("degree")
    orders = order_table - slot_count // 2
    angles = jnp.arange(slot_count, dtype=jnp.int32)
    phase_index = jnp.mod(orders[:, None] * angles[None, :], slot_count)
    radians = phase_index.astype(jnp.float32) * (2.0 * math.pi / slot_count)
    cosine = jnp.cos(radians)
    sine_table = jnp.sin(radians)
    magnitude = jnp.abs(orders)
    resident_degrees = degree_pos * local_deg + jnp.arange(local_deg, dtype=jnp.int32)
    owned_orders = lax.dynamic_slice_in_dim(magnitude, order_pos * local_ord, local_ord)
    grip_allowed = owned_orders[None, :] <= resident_degrees[:, None]
    selector = (jnp.arange(cand_count, dtype=jnp.int32)[:, None] == site_ids[None, :]).astype(
        jnp.bfloat16
    )
    chosen = jnp.dot(
        scene_coeffs.reshape(-1, cand_count), selector, preferred_element_type=jnp.float32
    )
    chosen = chosen.astype(jnp.bfloat16).reshape(
        2, scene_coeffs.shape[1], local_deg, local_ord, site_count
    )
    grip_real = jnp.concatenate([gripper_coeffs[0], gripper_coeffs[1]], axis=0)
    grip_imag = jnp.concatenate([-gripper_coeffs[1], gripper_coeffs[0]], axis=0)
    gripper_couple = jnp.stack([grip_real, grip_imag])
    columns_in = lax.all_gather(chosen, "order", axis=3, tiled=True)
    scene_joined = jnp.concatenate([columns_in[0], columns_in[1]], axis=0)
    product = jnp.einsum(
        "aonw,iaob->iobnw", scene_joined, gripper_couple, preferred_element_type=jnp.float32
    )
    permitted_mask = grip_allowed[:, :, None] & (
        magnitude[None, None, :] <= resident_degrees[:, None, None]
    )
    product = jnp.where(permitted_mask[None, :, :, :, None], product, jnp.float32(0.0)).astype(
        jnp.bfloat16
    )
    partial_value = jnp.einsum(
        "ylprs,lbpr->ysbpr", product, wigner, preferred_element_type=jnp.float32
    )
    summed = lax.psum_scatter(partial_value, "degree", scatter_dimension=2, tiled=True)
    phase_pair = jnp.concatenate([cosine, sine_table], axis=1)
    products = jnp.einsum(
        "xsbpm,mk->xsbpk", summed, phase_pair, precision=highest, preferred_element_type=jnp.float32
    )
    real_alpha = products[0, ..., :slot_count] - products[1, ..., slot_count:]
    imag_alpha = products[0, ..., slot_count:] + products[1, ..., :slot_count]
    stacked_parts = jnp.stack([real_alpha, imag_alpha])
    exchanged = lax.all_to_all(stacked_parts, "order", split_axis=4, concat_axis=3, tiled=True)
    first_term = jnp.einsum(
        "sbpa,pk->sbak", exchanged[0], cosine, precision=highest, preferred_element_type=jnp.float32
    )
    latter_addend = jnp.einsum(
        "sbpa,pk->sbak",
        exchanged[1],
        sine_table,
        precision=highest,
        preferred_element_type=jnp.float32,
    )
    return first_term - latter_addend


MESH = pl.DeviceIdType.MESH
F32, BF16 = jnp.float32, jnp.bfloat16
CHUNKS = 4
PIECES = (8, 8, 8, 8)
STAGED = 4
PLAN = (
    "s0 s1 s2 s3",
    "f0 f1 f2 f3",
    "x c0 p c1",
    "u0 c2 u1 c3",
    "r0 u2 r1 u3",
    "r2 t r3 v0",
    "v1 v2 v3 a",
)
UNITS = ((0, 8, (0,)), (8, 8, (1,)), (16, 8, (2,)), (24, 8, (3,)))
ROWS = 16
GROUP = 8


def cos_of(index, count):
    centred = jnp.bitwise_and(index + count // 2, count - 1) - count // 2
    half = centred.astype(F32) * F32(math.pi / count)
    sq = half * half
    poly = F32(-1.0 / 39916800.0)
    for coefficient in (1.0 / 362880.0, -1.0 / 5040.0, 1.0 / 120.0, -1.0 / 6.0, 1.0):
        poly = poly * sq + F32(coefficient)
    sine = poly * half
    return 1.0 - 2.0 * sine * sine


def split(value):
    high = value.astype(BF16)
    return high, (value - high.astype(F32)).astype(BF16)


def fused_kernel(
    scene_ref, site_ref, g_hbm, row_hbm, w_ref, out_ref, last_ref, wbuf, *scratch
):
    cands, scratch = scratch[: len(PIECES)], scratch[len(PIECES) :]
    fused_body(scene_ref, site_ref, g_hbm, row_hbm, w_ref, out_ref, last_ref, wbuf, cands, *scratch)


def fused_body(
    scene_ref, site_ref, g_hbm, row_hbm, w_ref, out_ref, last_ref, wbuf, cands,
    g_ref, row_ref, sbuf, prod, accbuf, rs_send, rs_recv, a_send, a_recv, halfacc,
    alpha_hi, alpha_lo, gamma_hi, gamma_lo, g32, col,
    in_sem, c_sem, w_sem, s_send_sem, s_recv_sem, r_send_sem, r_recv_sem, x_send_sem, x_recv_sem,
):
    me = lax.axis_index("order")
    deg = lax.axis_index("degree")
    HL, NBETA, P, M = wbuf.shape[2:]
    L = 2 * HL
    SL = 2 * M
    BO = NBETA // 2
    K = scene_ref.shape[0]
    first = me // 2
    second = 1 - first
    near = first * 2 + (1 - me % 2)
    per = HL // CHUNKS
    blocks = P // ROWS

    def w_copy(h, c):
        return pltpu.make_async_copy(
            w_ref.at[:, pl.ds(c * per, per), :, :, pl.ds(pl.multiple_of(h * M, M), M)],
            wbuf.at[h, :, pl.ds(c * per, per)],
            w_sem.at[h, c],
        )

    starts = [sum(PIECES[:i]) for i in range(len(PIECES))]

    def c_copy(c):
        return pltpu.make_async_copy(
            scene_ref.at[:, :, pl.ds(starts[c], PIECES[c])], cands[c], c_sem.at[c]
        )

    c_copy(0).start()
    g_copy = pltpu.make_async_copy(g_hbm, g_ref, in_sem.at[0])
    row_copy = pltpu.make_async_copy(row_hbm, row_ref, in_sem.at[1])
    row_copy.start()
    g_copy.start()
    for c in range(1, STAGED):
        c_copy(c).start()

    barrier = pltpu.get_barrier_semaphore()
    for off in (1, 2, 3):
        pl.semaphore_signal(barrier, 1, device_id={"order": (me + off) % 4}, device_id_type=MESH)
    pl.semaphore_signal(barrier, 1, device_id={"degree": 1 - deg}, device_id_type=MESH)

    site = site_ref[0]
    pick_row = lax.broadcasted_iota(jnp.int32, (K, K * GROUP), 0)
    pick_col = lax.broadcasted_iota(jnp.int32, (K, K * GROUP), 1)
    pick = (pick_col == pick_row * GROUP + site % GROUP).astype(F32).astype(BF16)

    def select(c):
        def step(i, carry):
            halves = []
            for part in range(2):
                tile = cands[c][:, part, i, site // GROUP].reshape(K * GROUP, P)
                halves.append(jnp.dot(pick, tile, preferred_element_type=F32))
            sbuf[me, starts[c] + i] = jnp.concatenate(halves, axis=1).astype(BF16)
            return carry

        c_copy(c).wait()
        lax.fori_loop(0, PIECES[c], step, 0, unroll=True)

    def hop(block, c, way):
        rows = pl.ds(starts[c], PIECES[c])
        return pltpu.make_async_remote_copy(
            src_ref=sbuf.at[block, rows],
            dst_ref=sbuf.at[block, rows],
            send_sem=s_send_sem.at[way, block, c], recv_sem=s_recv_sem.at[block, c],
            device_id={"order": me + 1 - 2 * way}, device_id_type=MESH,
        )

    def send_own(c):
        @pl.when(me < 3)
        def _():
            hop(me, c, 0).start()

        @pl.when(me > 0)
        def _():
            hop(me, c, 1).start()

    def prepare():
        row_copy.wait()
        for h in range(2):
            line = jnp.broadcast_to(row_ref[h].astype(F32), (M, M))
            col[h * M : (h + 1) * M, :] = jnp.transpose(line).astype(jnp.int32) - SL // 2
        g_copy.wait()
        real = g_ref[0].astype(F32).reshape(K // 2 * L, P)
        imag = g_ref[1].astype(F32).reshape(K // 2 * L, P)
        g32[: K // 2 * L] = jnp.concatenate([real, -imag], axis=1)
        g32[K // 2 * L :] = jnp.concatenate([imag, real], axis=1)
        accbuf[...] = jnp.zeros_like(accbuf)

    dims = (((0,), (0,)), ((), ()))

    def tables():
        quarter = SL // 4
        lane = lax.broadcasted_iota(jnp.int32, (M, M), 1)
        left = lane < P
        for h in range(2):
            orders = col[h * M : (h + 1) * M, :]
            upright, turned = [], []
            for t in range(4):
                at = slice(t * M, (t + 1) * M)
                phase = orders * (t * P + lane % P) - (lane // P) * quarter
                upright.append(cos_of(phase, SL))
                swapped = pltpu.roll(upright[t], P, 1)
                turned.append(jnp.where(left, -swapped, swapped))
                for x, value in ((0, upright[t]), (1, turned[t])):
                    hi, lo = split(value)
                    alpha_hi[h, x * M : (x + 1) * M, at] = hi
                    alpha_lo[h, x * M : (x + 1) * M, at] = lo
            for t in range(4):
                at = slice(t * M, (t + 1) * M)
                one = t % 2 * 2
                if t < 2:
                    value = jnp.where(left, upright[one], turned[one + 1])
                else:
                    value = jnp.where(left, turned[one], -upright[one + 1])
                hi, lo = split(value)
                gamma_hi[h * M : (h + 1) * M, at] = hi
                gamma_lo[h * M : (h + 1) * M, at] = lo

    def r_copy(h, blk):
        return pltpu.make_async_remote_copy(
            src_ref=rs_send.at[h, blk], dst_ref=rs_recv.at[h, blk],
            send_sem=r_send_sem.at[h, blk], recv_sem=r_recv_sem.at[h, blk],
            device_id={"degree": 1 - deg}, device_id_type=MESH,
        )

    def unit(h, start, size, last):
        mag_p = jnp.abs(col[pl.ds(pl.multiple_of(me * P, P), P), :])
        mag_m = jnp.abs(row_ref[h] - SL // 2)
        most = jnp.maximum(mag_p, jnp.broadcast_to(mag_m, (P, M)))
        most = jnp.concatenate([most, most], axis=0)
        for i in range(size):
            step = start + i
            b0, b1 = sbuf[2 * h, step], sbuf[2 * h + 1, step]
            low = jnp.concatenate([b0[:, :P], b1[:, :P]], axis=1)
            high = jnp.concatenate([b0[:, P:], b1[:, P:]], axis=1)
            for part, scene in ((0, low), (1, high)):
                l = step + part * HL
                grip = g32[pl.ds(l, K, stride=L), :].astype(BF16)
                value = lax.dot_general(grip, scene, dims, preferred_element_type=F32)
                value = jnp.where(most <= deg * L + l, value, F32(0.0))
                prod[part, i] = value.astype(BF16)

        def rows(blk, low, count):
            at = pl.multiple_of(blk * ROWS, ROWS)

            def degree_step(i, acc):
                acc = list(acc)
                for part in range(2):
                    pr = prod[part, i, pl.ds(at, ROWS), :].astype(F32)
                    pi = prod[part, i, pl.ds(at + P, ROWS), :].astype(F32)
                    for b in range(count):
                        w = wbuf[h, part, start + i, low + b, pl.ds(at, ROWS), :].astype(F32)
                        acc[2 * b] += pr * w
                        acc[2 * b + 1] += pi * w
                return tuple(acc)

            acc = tuple(accbuf[h, blk, low + n // 2, n % 2] for n in range(2 * count))
            acc = lax.fori_loop(0, size, degree_step, acc, unroll=2)
            for n in range(2 * count):
                accbuf[h, blk, low + n // 2, n % 2] = acc[n]

        def whole(blk, carry):
            rows(blk, 0, NBETA)
            return carry

        def given(blk, carry):
            rows(blk, (1 - deg) * BO, BO)
            rs_send[h, blk] = accbuf[h, blk, pl.ds((1 - deg) * BO, BO)].astype(BF16)
            r_copy(h, blk).start()
            return carry

        def kept(blk, carry):
            rows(blk, deg * BO, BO)
            return carry

        if last:
            lax.fori_loop(0, blocks, given, 0)
            lax.fori_loop(0, blocks, kept, 0)
        else:
            lax.fori_loop(0, blocks, whole, 0)

    def alpha(h, blk):
        r_copy(h, blk).wait_recv()
        total = accbuf[h, blk, pl.ds(deg * BO, BO)] + rs_recv[h, blk].astype(F32)
        total = jnp.concatenate(
            [total[:, 0].reshape(BO * ROWS, M), total[:, 1].reshape(BO * ROWS, M)], axis=1
        )
        hi, lo = split(total)
        value = jnp.dot(hi, alpha_hi[h], preferred_element_type=F32)
        value += jnp.dot(hi, alpha_lo[h], preferred_element_type=F32)
        value += jnp.dot(lo, alpha_hi[h], preferred_element_type=F32)
        return value

    across = lax.max(me - 1, 0) % 2
    middle = (me == 1) | (me == 2)
    other = me + 1 - 2 * across
    beyond = other + 1 - 2 * across

    def wait_block(block, c):
        hop(block, c, me // 3).wait_recv()

    def collect(c):
        wait_block(near, c)

        @pl.when(middle)
        def _():
            hop(near, c, across).start()
            wait_block(other, c)
            hop(other, c, 1 - across).start()

    def relay(c):
        @pl.when(middle)
        def _():
            wait_block(beyond, c)
            hop(beyond, c, 1 - across).start()

    def wait_second(i):
        @pl.when(jnp.logical_not(middle))
        def _():
            wait_block(second * 2, i)
            wait_block(second * 2 + 1, i)

    def own(i):
        select(i)
        if i == 0:
            pl.semaphore_wait(barrier, 4)
        send_own(i)

    def fetch_first(c):
        w_copy(first, c).start()

    def fetch_second():
        for c in range(CHUNKS):
            w_copy(second, c).start()

    def unit_first(c):
        w_copy(first, c).wait()
        unit(first, c * per, per, c == CHUNKS - 1)

    def unit_second(n):
        start, size, pieces = UNITS[n]
        for i in pieces:
            wait_second(i)
        if start % per == 0:
            w_copy(second, start // per).wait()
        unit(second, start, size, n == len(UNITS) - 1)

    def alpha_first():
        for blk in range(blocks):
            halfacc[blk] = alpha(first, blk)

    def stage(c):
        c_copy(c).start()

    acts = {
        "s": own, "c": collect, "r": relay, "f": fetch_first, "x": fetch_second, "p": prepare,
        "t": tables, "u": unit_first, "v": unit_second, "a": alpha_first, "k": stage,
    }
    for item in sum((part.split() for part in PLAN), []):
        acts[item[0]](*[int(item[1:])] if item[1:] else [])

    def x_copy(target, source, blk, off):
        return pltpu.make_async_remote_copy(
            src_ref=a_send.at[target, blk], dst_ref=a_recv.at[source, blk],
            send_sem=x_send_sem.at[off, blk], recv_sem=x_recv_sem.at[off, blk],
            device_id={"order": target}, device_id_type=MESH,
        )

    for blk in range(blocks):
        value = (halfacc[blk] + alpha(second, blk)).astype(BF16)
        for t in range(4):
            a_send[t, blk] = value[:, t * M : (t + 1) * M]
        for off in (3, 2, 1):
            far = jnp.where(me < 2, (me + off) % 4, (me - off + 4) % 4)
            x_copy(far, me, blk, (far - me + 4) % 4).start()
        a_recv[me, blk] = a_send[me, blk]

    def gamma(source):
        rows = pl.ds(pl.multiple_of(source * P, P), P)
        got = [
            jnp.concatenate(
                [a_recv[source, blk, b * ROWS : (b + 1) * ROWS, :] for blk in range(blocks)], axis=0
            )
            for b in range(BO)
        ]
        parts = [
            jnp.concatenate([piece[:, x * P : (x + 1) * P] for piece in got], axis=1)
            for x in range(2)
        ]
        left = jnp.concatenate(parts + parts, axis=0)
        right = jnp.concatenate(
            [
                table[rows, x * SL : (x + 1) * SL]
                for table in (gamma_hi, gamma_lo)
                for x in range(2)
            ],
            axis=0,
        )
        score = lax.dot_general(left, right, dims, preferred_element_type=F32)
        return score.reshape(BO, P, SL)

    out_ref[0] = gamma(me)
    for off in (1, 2, 3):
        source = jnp.where(me < 2, (me + off) % 4, (me - off + 4) % 4)
        for blk in range(blocks):
            x_copy(source, source, blk, (me - source + 4) % 4).wait_recv()
        if off < 3:
            out_ref[0] += gamma(source)
        else:
            last_ref[0] = gamma(source)

    for c in range(len(PIECES)):
        @pl.when(me < 3)
        def _():
            hop(me, c, 0).wait_send()

        @pl.when(me > 0)
        def _():
            hop(me, c, 1).wait_send()

        @pl.when(middle)
        def _():
            hop(near, c, across).wait_send()
            hop(other, c, 1 - across).wait_send()
            hop(beyond, c, 1 - across).wait_send()

    for blk in range(blocks):
        for off in (1, 2, 3):
            x_copy((me + off) % 4, me, blk, off).wait_send()
        r_copy(first, blk).wait_send()
        r_copy(second, blk).wait_send()


def fused_shards(scene_coeffs, site_ids, gripper_coeffs, order_table, wigner):
    L, NBETA, P, SL = wigner.shape
    M = SL // 2
    K = 2 * scene_coeffs.shape[1]
    BO = NBETA // 2
    NB = P // ROWS
    cand = scene_coeffs.shape[4]
    tall = jnp.transpose(scene_coeffs, (0, 1, 2, 4, 3))
    tall = tall.reshape(K, 2, L // 2, cand // GROUP, GROUP, P)
    vmem = pl.BlockSpec(memory_space=pltpu.VMEM)
    hbm = pl.BlockSpec(memory_space=pltpu.HBM)
    score, last = pl.pallas_call(
        fused_kernel,
        out_shape=[jax.ShapeDtypeStruct((1, BO, P, SL), F32)] * 2,
        in_specs=[hbm, pl.BlockSpec(memory_space=pltpu.SMEM), hbm, hbm, hbm],
        out_specs=[vmem, vmem],
        scratch_shapes=[
            pltpu.VMEM((2, 2, L // 2, NBETA, P, M), BF16),
            *[
                pltpu.VMEM((K, 2, size, cand // GROUP, GROUP, P), BF16) for size in PIECES
            ],
            pltpu.VMEM((2, K // 2, L, P), BF16),
            pltpu.VMEM((2, 1, M), jnp.int32),
            pltpu.VMEM((4, L // 2, K, 2 * P), BF16),
            pltpu.VMEM((2, L // 2 // CHUNKS, 2 * P, M), BF16),
            pltpu.VMEM((2, NB, NBETA, 2, ROWS, M), F32),
            pltpu.VMEM((2, NB, BO, 2, ROWS, M), BF16),
            pltpu.VMEM((2, NB, BO, 2, ROWS, M), BF16),
            pltpu.VMEM((4, NB, BO * ROWS, M), BF16),
            pltpu.VMEM((4, NB, BO * ROWS, M), BF16),
            pltpu.VMEM((NB, BO * ROWS, 2 * SL), F32),
            pltpu.VMEM((2, 2 * M, 2 * SL), BF16),
            pltpu.VMEM((2, 2 * M, 2 * SL), BF16),
            pltpu.VMEM((SL, 2 * SL), BF16),
            pltpu.VMEM((SL, 2 * SL), BF16),
            pltpu.VMEM((K * L, 2 * P), F32),
            pltpu.VMEM((SL, M), jnp.int32),
            pltpu.SemaphoreType.DMA((2,)),
            pltpu.SemaphoreType.DMA((len(PIECES),)),
            pltpu.SemaphoreType.DMA((2, CHUNKS)),
            pltpu.SemaphoreType.DMA((2, 4, len(PIECES))),
            pltpu.SemaphoreType.DMA((4, len(PIECES))),
            pltpu.SemaphoreType.DMA((2, NB)),
            pltpu.SemaphoreType.DMA((2, NB)),
            pltpu.SemaphoreType.DMA((4, NB)),
            pltpu.SemaphoreType.DMA((4, NB)),
        ],
        compiler_params=pltpu.CompilerParams(
            collective_id=0, has_side_effects=True, vmem_limit_bytes=48 * 1024 * 1024
        ),
    )(
        tall,
        site_ids,
        pltpu.with_memory_space_constraint(gripper_coeffs, pltpu.HBM),
        pltpu.with_memory_space_constraint(order_table.reshape(2, 1, M), pltpu.HBM),
        wigner.reshape(2, L // 2, NBETA, P, SL),
    )
    return score + last


def solution(mesh):
    fits = mesh.shape["order"] == 4 and mesh.shape["degree"] == 2 and mesh.shape["site"] == 4
    shards = fused_shards if fits else general_shards
    in_specs = (
        P(None, None, "degree", "order", None),
        P("site"),
        P(None, None, "degree", "order"),
        P(),
        P("degree", None, "order", None),
    )
    out_specs = P("site", "degree", "order", None)
    return jax.shard_map(shards, mesh=mesh, in_specs=in_specs, out_specs=out_specs, check_vma=False)
```

```python
import math

import jax
import jax.numpy as jnp
from jax import lax
from jax.experimental import pallas as pl
from jax.experimental.pallas import tpu as pltpu
from jax.sharding import PartitionSpec as P


def general_shards(scene_coeffs, site_ids, gripper_coeffs, order_table, wigner):
    highest = lax.Precision.HIGHEST
    slot_count = order_table.shape[0]
    local_deg = gripper_coeffs.shape[2]
    local_ord = gripper_coeffs.shape[3]
    cand_count = scene_coeffs.shape[4]
    site_count = site_ids.shape[0]
    order_pos = lax.axis_index("order")
    degree_pos = lax.axis_index("degree")
    orders = order_table - slot_count // 2
    angles = jnp.arange(slot_count, dtype=jnp.int32)
    phase_index = jnp.mod(orders[:, None] * angles[None, :], slot_count)
    radians = phase_index.astype(jnp.float32) * (2.0 * math.pi / slot_count)
    cosine = jnp.cos(radians)
    sine_table = jnp.sin(radians)
    magnitude = jnp.abs(orders)
    resident_degrees = degree_pos * local_deg + jnp.arange(local_deg, dtype=jnp.int32)
    owned_orders = lax.dynamic_slice_in_dim(magnitude, order_pos * local_ord, local_ord)
    grip_allowed = owned_orders[None, :] <= resident_degrees[:, None]
    selector = (jnp.arange(cand_count, dtype=jnp.int32)[:, None] == site_ids[None, :]).astype(
        jnp.bfloat16
    )
    chosen = jnp.dot(
        scene_coeffs.reshape(-1, cand_count), selector, preferred_element_type=jnp.float32
    )
    chosen = chosen.astype(jnp.bfloat16).reshape(
        2, scene_coeffs.shape[1], local_deg, local_ord, site_count
    )
    grip_real = jnp.concatenate([gripper_coeffs[0], gripper_coeffs[1]], axis=0)
    grip_imag = jnp.concatenate([-gripper_coeffs[1], gripper_coeffs[0]], axis=0)
    gripper_couple = jnp.stack([grip_real, grip_imag])
    columns_in = lax.all_gather(chosen, "order", axis=3, tiled=True)
    scene_joined = jnp.concatenate([columns_in[0], columns_in[1]], axis=0)
    product = jnp.einsum(
        "aonw,iaob->iobnw", scene_joined, gripper_couple, preferred_element_type=jnp.float32
    )
    permitted_mask = grip_allowed[:, :, None] & (
        magnitude[None, None, :] <= resident_degrees[:, None, None]
    )
    product = jnp.where(permitted_mask[None, :, :, :, None], product, jnp.float32(0.0)).astype(
        jnp.bfloat16
    )
    partial_value = jnp.einsum(
        "ylprs,lbpr->ysbpr", product, wigner, preferred_element_type=jnp.float32
    )
    summed = lax.psum_scatter(partial_value, "degree", scatter_dimension=2, tiled=True)
    phase_pair = jnp.concatenate([cosine, sine_table], axis=1)
    products = jnp.einsum(
        "xsbpm,mk->xsbpk", summed, phase_pair, precision=highest, preferred_element_type=jnp.float32
    )
    real_alpha = products[0, ..., :slot_count] - products[1, ..., slot_count:]
    imag_alpha = products[0, ..., slot_count:] + products[1, ..., :slot_count]
    stacked_parts = jnp.stack([real_alpha, imag_alpha])
    exchanged = lax.all_to_all(stacked_parts, "order", split_axis=4, concat_axis=3, tiled=True)
    first_term = jnp.einsum(
        "sbpa,pk->sbak", exchanged[0], cosine, precision=highest, preferred_element_type=jnp.float32
    )
    latter_addend = jnp.einsum(
        "sbpa,pk->sbak",
        exchanged[1],
        sine_table,
        precision=highest,
        preferred_element_type=jnp.float32,
    )
    return first_term - latter_addend


MESH = pl.DeviceIdType.MESH
F32, BF16 = jnp.float32, jnp.bfloat16
CHUNKS = 4
PIECES = (8, 8, 8, 8)
STAGED = 4
PLAN = (
    "s0 s1 s2 s3",
    "f0 f1 f2 f3",
    "x c0 p c1",
    "u0 c2 u1 r0",
    "c3 u2 r1 u3",
    "r2 t r3 v0",
    "v1 v2 v3 a",
)
UNITS = ((0, 8, (0,)), (8, 8, (1,)), (16, 8, (2,)), (24, 8, (3,)))
ROWS = 16
GROUP = 8


def cos_of(index, count):
    centred = jnp.bitwise_and(index + count // 2, count - 1) - count // 2
    half = centred.astype(F32) * F32(math.pi / count)
    sq = half * half
    poly = F32(-1.0 / 39916800.0)
    for coefficient in (1.0 / 362880.0, -1.0 / 5040.0, 1.0 / 120.0, -1.0 / 6.0, 1.0):
        poly = poly * sq + F32(coefficient)
    sine = poly * half
    return 1.0 - 2.0 * sine * sine


def split(value):
    high = value.astype(BF16)
    return high, (value - high.astype(F32)).astype(BF16)


def fused_kernel(
    scene_ref, site_ref, g_hbm, row_hbm, w_ref, out_ref, last_ref, wbuf, *scratch
):
    cands, scratch = scratch[: len(PIECES)], scratch[len(PIECES) :]
    fused_body(scene_ref, site_ref, g_hbm, row_hbm, w_ref, out_ref, last_ref, wbuf, cands, *scratch)


def fused_body(
    scene_ref, site_ref, g_hbm, row_hbm, w_ref, out_ref, last_ref, wbuf, cands,
    g_ref, row_ref, sbuf, prod, accbuf, rs_send, rs_recv, a_send, a_recv, halfacc,
    alpha_hi, alpha_lo, gamma_hi, gamma_lo, g32, col,
    in_sem, c_sem, w_sem, s_send_sem, s_recv_sem, r_send_sem, r_recv_sem, x_send_sem, x_recv_sem,
):
    me = lax.axis_index("order")
    deg = lax.axis_index("degree")
    HL, NBETA, P, M = wbuf.shape[2:]
    L = 2 * HL
    SL = 2 * M
    BO = NBETA // 2
    K = scene_ref.shape[0]
    first = me // 2
    second = 1 - first
    near = first * 2 + (1 - me % 2)
    per = HL // CHUNKS
    blocks = P // ROWS

    def w_copy(h, c):
        return pltpu.make_async_copy(
            w_ref.at[:, pl.ds(c * per, per), :, :, pl.ds(pl.multiple_of(h * M, M), M)],
            wbuf.at[h, :, pl.ds(c * per, per)],
            w_sem.at[h, c],
        )

    starts = [sum(PIECES[:i]) for i in range(len(PIECES))]

    def c_copy(c):
        return pltpu.make_async_copy(
            scene_ref.at[:, :, pl.ds(starts[c], PIECES[c])], cands[c], c_sem.at[c]
        )

    c_copy(0).start()
    g_copy = pltpu.make_async_copy(g_hbm, g_ref, in_sem.at[0])
    row_copy = pltpu.make_async_copy(row_hbm, row_ref, in_sem.at[1])
    row_copy.start()
    g_copy.start()
    for c in range(1, STAGED):
        c_copy(c).start()

    barrier = pltpu.get_barrier_semaphore()
    for off in (1, 2, 3):
        pl.semaphore_signal(barrier, 1, device_id={"order": (me + off) % 4}, device_id_type=MESH)
    pl.semaphore_signal(barrier, 1, device_id={"degree": 1 - deg}, device_id_type=MESH)

    site = site_ref[0]
    pick_row = lax.broadcasted_iota(jnp.int32, (K, K * GROUP), 0)
    pick_col = lax.broadcasted_iota(jnp.int32, (K, K * GROUP), 1)
    pick = (pick_col == pick_row * GROUP + site % GROUP).astype(F32).astype(BF16)

    def select(c):
        def step(i, carry):
            halves = []
            for part in range(2):
                tile = cands[c][:, part, i, site // GROUP].reshape(K * GROUP, P)
                halves.append(jnp.dot(pick, tile, preferred_element_type=F32))
            sbuf[me, starts[c] + i] = jnp.concatenate(halves, axis=1).astype(BF16)
            return carry

        c_copy(c).wait()
        lax.fori_loop(0, PIECES[c], step, 0, unroll=True)

    def hop(block, c, way):
        rows = pl.ds(starts[c], PIECES[c])
        return pltpu.make_async_remote_copy(
            src_ref=sbuf.at[block, rows],
            dst_ref=sbuf.at[block, rows],
            send_sem=s_send_sem.at[way, block, c], recv_sem=s_recv_sem.at[block, c],
            device_id={"order": me + 1 - 2 * way}, device_id_type=MESH,
        )

    def send_own(c):
        @pl.when(me < 3)
        def _():
            hop(me, c, 0).start()

        @pl.when(me > 0)
        def _():
            hop(me, c, 1).start()

    def prepare():
        row_copy.wait()
        for h in range(2):
            line = jnp.broadcast_to(row_ref[h].astype(F32), (M, M))
            col[h * M : (h + 1) * M, :] = jnp.transpose(line).astype(jnp.int32) - SL // 2
        g_copy.wait()
        real = g_ref[0].astype(F32).reshape(K // 2 * L, P)
        imag = g_ref[1].astype(F32).reshape(K // 2 * L, P)
        g32[: K // 2 * L] = jnp.concatenate([real, -imag], axis=1)
        g32[K // 2 * L :] = jnp.concatenate([imag, real], axis=1)
        accbuf[...] = jnp.zeros_like(accbuf)

    dims = (((0,), (0,)), ((), ()))

    def tables():
        quarter = SL // 4
        lane = lax.broadcasted_iota(jnp.int32, (M, M), 1)
        left = lane < P
        for h in range(2):
            orders = col[h * M : (h + 1) * M, :]
            upright, turned = [], []
            for t in range(4):
                at = slice(t * M, (t + 1) * M)
                phase = orders * (t * P + lane % P) - (lane // P) * quarter
                upright.append(cos_of(phase, SL))
                swapped = pltpu.roll(upright[t], P, 1)
                turned.append(jnp.where(left, -swapped, swapped))
                for x, value in ((0, upright[t]), (1, turned[t])):
                    hi, lo = split(value)
                    alpha_hi[h, x * M : (x + 1) * M, at] = hi
                    alpha_lo[h, x * M : (x + 1) * M, at] = lo
            for t in range(4):
                at = slice(t * M, (t + 1) * M)
                one = t % 2 * 2
                if t < 2:
                    value = jnp.where(left, upright[one], turned[one + 1])
                else:
                    value = jnp.where(left, turned[one], -upright[one + 1])
                hi, lo = split(value)
                gamma_hi[h * M : (h + 1) * M, at] = hi
                gamma_lo[h * M : (h + 1) * M, at] = lo

    def r_copy(h, blk):
        return pltpu.make_async_remote_copy(
            src_ref=rs_send.at[h, blk], dst_ref=rs_recv.at[h, blk],
            send_sem=r_send_sem.at[h, blk], recv_sem=r_recv_sem.at[h, blk],
            device_id={"degree": 1 - deg}, device_id_type=MESH,
        )

    def unit(h, start, size, last):
        mag_p = jnp.abs(col[pl.ds(pl.multiple_of(me * P, P), P), :])
        mag_m = jnp.abs(row_ref[h] - SL // 2)
        most = jnp.maximum(mag_p, jnp.broadcast_to(mag_m, (P, M)))
        most = jnp.concatenate([most, most], axis=0)
        for i in range(size):
            step = start + i
            b0, b1 = sbuf[2 * h, step], sbuf[2 * h + 1, step]
            low = jnp.concatenate([b0[:, :P], b1[:, :P]], axis=1)
            high = jnp.concatenate([b0[:, P:], b1[:, P:]], axis=1)
            for part, scene in ((0, low), (1, high)):
                l = step + part * HL
                grip = g32[pl.ds(l, K, stride=L), :].astype(BF16)
                value = lax.dot_general(grip, scene, dims, preferred_element_type=F32)
                value = jnp.where(most <= deg * L + l, value, F32(0.0))
                prod[part, i] = value.astype(BF16)

        def rows(blk, low, count):
            at = pl.multiple_of(blk * ROWS, ROWS)

            def degree_step(i, acc):
                acc = list(acc)
                for part in range(2):
                    pr = prod[part, i, pl.ds(at, ROWS), :].astype(F32)
                    pi = prod[part, i, pl.ds(at + P, ROWS), :].astype(F32)
                    for b in range(count):
                        w = wbuf[h, part, start + i, low + b, pl.ds(at, ROWS), :].astype(F32)
                        acc[2 * b] += pr * w
                        acc[2 * b + 1] += pi * w
                return tuple(acc)

            acc = tuple(accbuf[h, blk, low + n // 2, n % 2] for n in range(2 * count))
            acc = lax.fori_loop(0, size, degree_step, acc, unroll=2)
            for n in range(2 * count):
                accbuf[h, blk, low + n // 2, n % 2] = acc[n]

        def whole(blk, carry):
            rows(blk, 0, NBETA)
            return carry

        def given(blk, carry):
            rows(blk, (1 - deg) * BO, BO)
            rs_send[h, blk] = accbuf[h, blk, pl.ds((1 - deg) * BO, BO)].astype(BF16)
            r_copy(h, blk).start()
            return carry

        def kept(blk, carry):
            rows(blk, deg * BO, BO)
            return carry

        if last:
            lax.fori_loop(0, blocks, given, 0)
            lax.fori_loop(0, blocks, kept, 0)
        else:
            lax.fori_loop(0, blocks, whole, 0)

    def alpha(h, blk):
        r_copy(h, blk).wait_recv()
        total = accbuf[h, blk, pl.ds(deg * BO, BO)] + rs_recv[h, blk].astype(F32)
        total = jnp.concatenate(
            [total[:, 0].reshape(BO * ROWS, M), total[:, 1].reshape(BO * ROWS, M)], axis=1
        )
        hi, lo = split(total)
        value = jnp.dot(hi, alpha_hi[h], preferred_element_type=F32)
        value += jnp.dot(hi, alpha_lo[h], preferred_element_type=F32)
        value += jnp.dot(lo, alpha_hi[h], preferred_element_type=F32)
        return value

    across = lax.max(me - 1, 0) % 2
    middle = (me == 1) | (me == 2)
    other = me + 1 - 2 * across
    beyond = other + 1 - 2 * across

    def wait_block(block, c):
        hop(block, c, me // 3).wait_recv()

    def collect(c):
        wait_block(near, c)

        @pl.when(middle)
        def _():
            hop(near, c, across).start()
            wait_block(other, c)
            hop(other, c, 1 - across).start()

    def relay(c):
        @pl.when(middle)
        def _():
            wait_block(beyond, c)
            hop(beyond, c, 1 - across).start()

    def wait_second(i):
        @pl.when(jnp.logical_not(middle))
        def _():
            wait_block(second * 2, i)
            wait_block(second * 2 + 1, i)

    def own(i):
        select(i)
        if i == 0:
            pl.semaphore_wait(barrier, 4)
        send_own(i)

    def fetch_first(c):
        w_copy(first, c).start()

    def fetch_second():
        for c in range(CHUNKS):
            w_copy(second, c).start()

    def unit_first(c):
        w_copy(first, c).wait()
        unit(first, c * per, per, c == CHUNKS - 1)

    def unit_second(n):
        start, size, pieces = UNITS[n]
        for i in pieces:
            wait_second(i)
        if start % per == 0:
            w_copy(second, start // per).wait()
        unit(second, start, size, n == len(UNITS) - 1)

    def alpha_first():
        for blk in range(blocks):
            halfacc[blk] = alpha(first, blk)

    def stage(c):
        c_copy(c).start()

    acts = {
        "s": own, "c": collect, "r": relay, "f": fetch_first, "x": fetch_second, "p": prepare,
        "t": tables, "u": unit_first, "v": unit_second, "a": alpha_first, "k": stage,
    }
    for item in sum((part.split() for part in PLAN), []):
        acts[item[0]](*[int(item[1:])] if item[1:] else [])

    def x_copy(target, source, blk, off):
        return pltpu.make_async_remote_copy(
            src_ref=a_send.at[target, blk], dst_ref=a_recv.at[source, blk],
            send_sem=x_send_sem.at[off, blk], recv_sem=x_recv_sem.at[off, blk],
            device_id={"order": target}, device_id_type=MESH,
        )

    for c in range(len(PIECES)):
        @pl.when(me < 3)
        def _():
            hop(me, c, 0).wait_send()

        @pl.when(me > 0)
        def _():
            hop(me, c, 1).wait_send()

        @pl.when(middle)
        def _():
            hop(near, c, across).wait_send()
            hop(other, c, 1 - across).wait_send()
            hop(beyond, c, 1 - across).wait_send()

    for blk in range(blocks):
        value = (halfacc[blk] + alpha(second, blk)).astype(BF16)
        for t in range(4):
            a_send[t, blk] = value[:, t * M : (t + 1) * M]
        for off in (3, 2, 1):
            far = jnp.where(me < 2, (me + off) % 4, (me - off + 4) % 4)
            x_copy(far, me, blk, (far - me + 4) % 4).start()
        a_recv[me, blk] = a_send[me, blk]

    def gamma(source):
        rows = pl.ds(pl.multiple_of(source * P, P), P)
        got = [
            jnp.concatenate(
                [a_recv[source, blk, b * ROWS : (b + 1) * ROWS, :] for blk in range(blocks)], axis=0
            )
            for b in range(BO)
        ]
        parts = [
            jnp.concatenate([piece[:, x * P : (x + 1) * P] for piece in got], axis=1)
            for x in range(2)
        ]
        left = jnp.concatenate(parts + parts, axis=0)
        right = jnp.concatenate(
            [
                table[rows, x * SL : (x + 1) * SL]
                for table in (gamma_hi, gamma_lo)
                for x in range(2)
            ],
            axis=0,
        )
        score = lax.dot_general(left, right, dims, preferred_element_type=F32)
        return score.reshape(BO, P, SL)

    out_ref[0] = gamma(me)
    for off in (1, 2, 3):
        source = jnp.where(me < 2, (me + off) % 4, (me - off + 4) % 4)
        if off == 3:
            for blk in range(blocks):
                for away in (1, 2, 3):
                    x_copy((me + away) % 4, me, blk, away).wait_send()
                r_copy(first, blk).wait_send()
                r_copy(second, blk).wait_send()
        for blk in range(blocks):
            x_copy(source, source, blk, (me - source + 4) % 4).wait_recv()
        if off < 3:
            out_ref[0] += gamma(source)
        else:
            last_ref[0] = gamma(source)


def fused_shards(scene_coeffs, site_ids, gripper_coeffs, order_table, wigner):
    L, NBETA, P, SL = wigner.shape
    M = SL // 2
    K = 2 * scene_coeffs.shape[1]
    BO = NBETA // 2
    NB = P // ROWS
    cand = scene_coeffs.shape[4]
    tall = jnp.transpose(scene_coeffs, (0, 1, 2, 4, 3))
    tall = tall.reshape(K, 2, L // 2, cand // GROUP, GROUP, P)
    vmem = pl.BlockSpec(memory_space=pltpu.VMEM)
    hbm = pl.BlockSpec(memory_space=pltpu.HBM)
    score, last = pl.pallas_call(
        fused_kernel,
        out_shape=[jax.ShapeDtypeStruct((1, BO, P, SL), F32)] * 2,
        in_specs=[hbm, pl.BlockSpec(memory_space=pltpu.SMEM), hbm, hbm, hbm],
        out_specs=[vmem, vmem],
        scratch_shapes=[
            pltpu.VMEM((2, 2, L // 2, NBETA, P, M), BF16),
            *[
                pltpu.VMEM((K, 2, size, cand // GROUP, GROUP, P), BF16) for size in PIECES
            ],
            pltpu.VMEM((2, K // 2, L, P), BF16),
            pltpu.VMEM((2, 1, M), jnp.int32),
            pltpu.VMEM((4, L // 2, K, 2 * P), BF16),
            pltpu.VMEM((2, L // 2 // CHUNKS, 2 * P, M), BF16),
            pltpu.VMEM((2, NB, NBETA, 2, ROWS, M), F32),
            pltpu.VMEM((2, NB, BO, 2, ROWS, M), BF16),
            pltpu.VMEM((2, NB, BO, 2, ROWS, M), BF16),
            pltpu.VMEM((4, NB, BO * ROWS, M), BF16),
            pltpu.VMEM((4, NB, BO * ROWS, M), BF16),
            pltpu.VMEM((NB, BO * ROWS, 2 * SL), F32),
            pltpu.VMEM((2, 2 * M, 2 * SL), BF16),
            pltpu.VMEM((2, 2 * M, 2 * SL), BF16),
            pltpu.VMEM((SL, 2 * SL), BF16),
            pltpu.VMEM((SL, 2 * SL), BF16),
            pltpu.VMEM((K * L, 2 * P), F32),
            pltpu.VMEM((SL, M), jnp.int32),
            pltpu.SemaphoreType.DMA((2,)),
            pltpu.SemaphoreType.DMA((len(PIECES),)),
            pltpu.SemaphoreType.DMA((2, CHUNKS)),
            pltpu.SemaphoreType.DMA((2, 4, len(PIECES))),
            pltpu.SemaphoreType.DMA((4, len(PIECES))),
            pltpu.SemaphoreType.DMA((2, NB)),
            pltpu.SemaphoreType.DMA((2, NB)),
            pltpu.SemaphoreType.DMA((4, NB)),
            pltpu.SemaphoreType.DMA((4, NB)),
        ],
        compiler_params=pltpu.CompilerParams(
            collective_id=0, has_side_effects=True, vmem_limit_bytes=48 * 1024 * 1024
        ),
    )(
        tall,
        site_ids,
        pltpu.with_memory_space_constraint(gripper_coeffs, pltpu.HBM),
        pltpu.with_memory_space_constraint(order_table.reshape(2, 1, M), pltpu.HBM),
        wigner.reshape(2, L // 2, NBETA, P, SL),
    )
    return score + last


def solution(mesh):
    fits = mesh.shape["order"] == 4 and mesh.shape["degree"] == 2 and mesh.shape["site"] == 4
    shards = fused_shards if fits else general_shards
    in_specs = (
        P(None, None, "degree", "order", None),
        P("site"),
        P(None, None, "degree", "order"),
        P(),
        P("degree", None, "order", None),
    )
    out_specs = P("site", "degree", "order", None)
    return jax.shard_map(shards, mesh=mesh, in_specs=in_specs, out_specs=out_specs, check_vma=False)
```

```python
import math

import jax
import jax.numpy as jnp
from jax import lax
from jax.experimental import pallas as pl
from jax.experimental.pallas import tpu as pltpu
from jax.sharding import PartitionSpec as P


def general_shards(scene_coeffs, site_ids, gripper_coeffs, order_table, wigner):
    highest = lax.Precision.HIGHEST
    slot_count = order_table.shape[0]
    local_deg = gripper_coeffs.shape[2]
    local_ord = gripper_coeffs.shape[3]
    cand_count = scene_coeffs.shape[4]
    site_count = site_ids.shape[0]
    order_pos = lax.axis_index("order")
    degree_pos = lax.axis_index("degree")
    orders = order_table - slot_count // 2
    angles = jnp.arange(slot_count, dtype=jnp.int32)
    phase_index = jnp.mod(orders[:, None] * angles[None, :], slot_count)
    radians = phase_index.astype(jnp.float32) * (2.0 * math.pi / slot_count)
    cosine = jnp.cos(radians)
    sine_table = jnp.sin(radians)
    magnitude = jnp.abs(orders)
    resident_degrees = degree_pos * local_deg + jnp.arange(local_deg, dtype=jnp.int32)
    owned_orders = lax.dynamic_slice_in_dim(magnitude, order_pos * local_ord, local_ord)
    grip_allowed = owned_orders[None, :] <= resident_degrees[:, None]
    selector = (jnp.arange(cand_count, dtype=jnp.int32)[:, None] == site_ids[None, :]).astype(
        jnp.bfloat16
    )
    chosen = jnp.dot(
        scene_coeffs.reshape(-1, cand_count), selector, preferred_element_type=jnp.float32
    )
    chosen = chosen.astype(jnp.bfloat16).reshape(
        2, scene_coeffs.shape[1], local_deg, local_ord, site_count
    )
    grip_real = jnp.concatenate([gripper_coeffs[0], gripper_coeffs[1]], axis=0)
    grip_imag = jnp.concatenate([-gripper_coeffs[1], gripper_coeffs[0]], axis=0)
    gripper_couple = jnp.stack([grip_real, grip_imag])
    columns_in = lax.all_gather(chosen, "order", axis=3, tiled=True)
    scene_joined = jnp.concatenate([columns_in[0], columns_in[1]], axis=0)
    product = jnp.einsum(
        "aonw,iaob->iobnw", scene_joined, gripper_couple, preferred_element_type=jnp.float32
    )
    permitted_mask = grip_allowed[:, :, None] & (
        magnitude[None, None, :] <= resident_degrees[:, None, None]
    )
    product = jnp.where(permitted_mask[None, :, :, :, None], product, jnp.float32(0.0)).astype(
        jnp.bfloat16
    )
    partial_value = jnp.einsum(
        "ylprs,lbpr->ysbpr", product, wigner, preferred_element_type=jnp.float32
    )
    summed = lax.psum_scatter(partial_value, "degree", scatter_dimension=2, tiled=True)
    phase_pair = jnp.concatenate([cosine, sine_table], axis=1)
    products = jnp.einsum(
        "xsbpm,mk->xsbpk", summed, phase_pair, precision=highest, preferred_element_type=jnp.float32
    )
    real_alpha = products[0, ..., :slot_count] - products[1, ..., slot_count:]
    imag_alpha = products[0, ..., slot_count:] + products[1, ..., :slot_count]
    stacked_parts = jnp.stack([real_alpha, imag_alpha])
    exchanged = lax.all_to_all(stacked_parts, "order", split_axis=4, concat_axis=3, tiled=True)
    first_term = jnp.einsum(
        "sbpa,pk->sbak", exchanged[0], cosine, precision=highest, preferred_element_type=jnp.float32
    )
    latter_addend = jnp.einsum(
        "sbpa,pk->sbak",
        exchanged[1],
        sine_table,
        precision=highest,
        preferred_element_type=jnp.float32,
    )
    return first_term - latter_addend


MESH = pl.DeviceIdType.MESH
F32, BF16 = jnp.float32, jnp.bfloat16
CHUNKS = 4
PIECES = (8, 8, 8, 8)
STAGED = 4
PLAN = (
    "s0 s1 s2 s3",
    "f0 f1 f2 f3",
    "x c0 p c1",
    "u0 c2 u1 r0",
    "c3 u2 r1 u3",
    "r2 t r3 v0",
    "v1 v2 v3 a",
)
UNITS = ((0, 8, (0,)), (8, 8, (1,)), (16, 8, (2,)), (24, 8, (3,)))
ROWS = 16
GROUP = 8


def cos_of(index, count):
    centred = jnp.bitwise_and(index + count // 2, count - 1) - count // 2
    half = centred.astype(F32) * F32(math.pi / count)
    sq = half * half
    poly = F32(-1.0 / 39916800.0)
    for coefficient in (1.0 / 362880.0, -1.0 / 5040.0, 1.0 / 120.0, -1.0 / 6.0, 1.0):
        poly = poly * sq + F32(coefficient)
    sine = poly * half
    return 1.0 - 2.0 * sine * sine


def split(value):
    high = value.astype(BF16)
    return high, (value - high.astype(F32)).astype(BF16)


def fused_kernel(
    scene_ref, site_ref, g_hbm, row_hbm, w_ref, out_ref, last_ref, wbuf, *scratch
):
    cands, scratch = scratch[: len(PIECES)], scratch[len(PIECES) :]
    fused_body(scene_ref, site_ref, g_hbm, row_hbm, w_ref, out_ref, last_ref, wbuf, cands, *scratch)


def fused_body(
    scene_ref, site_ref, g_hbm, row_hbm, w_ref, out_ref, last_ref, wbuf, cands,
    g_ref, row_ref, sbuf, prod, accbuf, rs_send, rs_recv, a_send, a_recv, halfacc,
    alpha_hi, alpha_lo, gamma_hi, gamma_lo, g32, col,
    in_sem, c_sem, w_sem, s_send_sem, s_recv_sem, r_send_sem, r_recv_sem, x_send_sem, x_recv_sem,
):
    me = lax.axis_index("order")
    deg = lax.axis_index("degree")
    HL, NBETA, P, M = wbuf.shape[2:]
    L = 2 * HL
    SL = 2 * M
    BO = NBETA // 2
    K = scene_ref.shape[0]
    first = me // 2
    second = 1 - first
    near = first * 2 + (1 - me % 2)
    per = HL // CHUNKS
    blocks = P // ROWS

    def w_copy(h, c):
        return pltpu.make_async_copy(
            w_ref.at[:, pl.ds(c * per, per), :, :, pl.ds(pl.multiple_of(h * M, M), M)],
            wbuf.at[h, :, pl.ds(c * per, per)],
            w_sem.at[h, c],
        )

    starts = [sum(PIECES[:i]) for i in range(len(PIECES))]

    def c_copy(c):
        return pltpu.make_async_copy(
            scene_ref.at[:, :, pl.ds(starts[c], PIECES[c])], cands[c], c_sem.at[c]
        )

    barrier = pltpu.get_barrier_semaphore()
    for off in (1, 2, 3):
        pl.semaphore_signal(barrier, 1, device_id={"order": (me + off) % 4}, device_id_type=MESH)
    pl.semaphore_signal(barrier, 1, device_id={"degree": 1 - deg}, device_id_type=MESH)

    c_copy(0).start()
    g_copy = pltpu.make_async_copy(g_hbm, g_ref, in_sem.at[0])
    row_copy = pltpu.make_async_copy(row_hbm, row_ref, in_sem.at[1])
    row_copy.start()
    g_copy.start()
    for c in range(1, STAGED):
        c_copy(c).start()

    site = site_ref[0]
    pick_row = lax.broadcasted_iota(jnp.int32, (K, K * GROUP), 0)
    pick_col = lax.broadcasted_iota(jnp.int32, (K, K * GROUP), 1)
    pick = (pick_col == pick_row * GROUP + site % GROUP).astype(F32).astype(BF16)

    def select(c):
        def step(i, carry):
            halves = []
            for part in range(2):
                tile = cands[c][:, part, i, site // GROUP].reshape(K * GROUP, P)
                halves.append(jnp.dot(pick, tile, preferred_element_type=F32))
            sbuf[me, starts[c] + i] = jnp.concatenate(halves, axis=1).astype(BF16)
            return carry

        c_copy(c).wait()
        lax.fori_loop(0, PIECES[c], step, 0, unroll=True)

    def hop(block, c, way):
        rows = pl.ds(starts[c], PIECES[c])
        return pltpu.make_async_remote_copy(
            src_ref=sbuf.at[block, rows],
            dst_ref=sbuf.at[block, rows],
            send_sem=s_send_sem.at[way, block, c], recv_sem=s_recv_sem.at[block, c],
            device_id={"order": me + 1 - 2 * way}, device_id_type=MESH,
        )

    def send_own(c):
        @pl.when(me < 3)
        def _():
            hop(me, c, 0).start()

        @pl.when(me > 0)
        def _():
            hop(me, c, 1).start()

    def prepare():
        row_copy.wait()
        for h in range(2):
            line = jnp.broadcast_to(row_ref[h].astype(F32), (M, M))
            col[h * M : (h + 1) * M, :] = jnp.transpose(line).astype(jnp.int32) - SL // 2
        g_copy.wait()
        real = g_ref[0].astype(F32).reshape(K // 2 * L, P)
        imag = g_ref[1].astype(F32).reshape(K // 2 * L, P)
        g32[: K // 2 * L] = jnp.concatenate([real, -imag], axis=1)
        g32[K // 2 * L :] = jnp.concatenate([imag, real], axis=1)
        accbuf[...] = jnp.zeros_like(accbuf)

    dims = (((0,), (0,)), ((), ()))

    def tables():
        quarter = SL // 4
        lane = lax.broadcasted_iota(jnp.int32, (M, M), 1)
        left = lane < P
        for h in range(2):
            orders = col[h * M : (h + 1) * M, :]
            upright, turned = [], []
            for t in range(4):
                at = slice(t * M, (t + 1) * M)
                phase = orders * (t * P + lane % P) - (lane // P) * quarter
                upright.append(cos_of(phase, SL))
                swapped = pltpu.roll(upright[t], P, 1)
                turned.append(jnp.where(left, -swapped, swapped))
                for x, value in ((0, upright[t]), (1, turned[t])):
                    hi, lo = split(value)
                    alpha_hi[h, x * M : (x + 1) * M, at] = hi
                    alpha_lo[h, x * M : (x + 1) * M, at] = lo
            for t in range(4):
                at = slice(t * M, (t + 1) * M)
                one = t % 2 * 2
                if t < 2:
                    value = jnp.where(left, upright[one], turned[one + 1])
                else:
                    value = jnp.where(left, turned[one], -upright[one + 1])
                hi, lo = split(value)
                gamma_hi[h * M : (h + 1) * M, at] = hi
                gamma_lo[h * M : (h + 1) * M, at] = lo

    def r_copy(h, blk):
        return pltpu.make_async_remote_copy(
            src_ref=rs_send.at[h, blk], dst_ref=rs_recv.at[h, blk],
            send_sem=r_send_sem.at[h, blk], recv_sem=r_recv_sem.at[h, blk],
            device_id={"degree": 1 - deg}, device_id_type=MESH,
        )

    def unit(h, start, size, last):
        mag_p = jnp.abs(col[pl.ds(pl.multiple_of(me * P, P), P), :])
        mag_m = jnp.abs(row_ref[h] - SL // 2)
        most = jnp.maximum(mag_p, jnp.broadcast_to(mag_m, (P, M)))
        most = jnp.concatenate([most, most], axis=0)
        for i in range(size):
            step = start + i
            b0, b1 = sbuf[2 * h, step], sbuf[2 * h + 1, step]
            low = jnp.concatenate([b0[:, :P], b1[:, :P]], axis=1)
            high = jnp.concatenate([b0[:, P:], b1[:, P:]], axis=1)
            for part, scene in ((0, low), (1, high)):
                l = step + part * HL
                grip = g32[pl.ds(l, K, stride=L), :].astype(BF16)
                value = lax.dot_general(grip, scene, dims, preferred_element_type=F32)
                value = jnp.where(most <= deg * L + l, value, F32(0.0))
                prod[part, i] = value.astype(BF16)

        def rows(blk, low, count):
            at = pl.multiple_of(blk * ROWS, ROWS)

            def degree_step(i, acc):
                acc = list(acc)
                for part in range(2):
                    pr = prod[part, i, pl.ds(at, ROWS), :].astype(F32)
                    pi = prod[part, i, pl.ds(at + P, ROWS), :].astype(F32)
                    for b in range(count):
                        w = wbuf[h, part, start + i, low + b, pl.ds(at, ROWS), :].astype(F32)
                        acc[2 * b] += pr * w
                        acc[2 * b + 1] += pi * w
                return tuple(acc)

            acc = tuple(accbuf[h, blk, low + n // 2, n % 2] for n in range(2 * count))
            acc = lax.fori_loop(0, size, degree_step, acc, unroll=4)
            for n in range(2 * count):
                accbuf[h, blk, low + n // 2, n % 2] = acc[n]

        def whole(blk, carry):
            rows(blk, 0, NBETA)
            return carry

        def given(blk, carry):
            rows(blk, (1 - deg) * BO, BO)
            rs_send[h, blk] = accbuf[h, blk, pl.ds((1 - deg) * BO, BO)].astype(BF16)
            r_copy(h, blk).start()
            return carry

        def kept(blk, carry):
            rows(blk, deg * BO, BO)
            return carry

        if last:
            lax.fori_loop(0, blocks, given, 0)
            lax.fori_loop(0, blocks, kept, 0)
        else:
            lax.fori_loop(0, blocks, whole, 0)

    def alpha(h, blk):
        r_copy(h, blk).wait_recv()
        total = accbuf[h, blk, pl.ds(deg * BO, BO)] + rs_recv[h, blk].astype(F32)
        total = jnp.concatenate(
            [total[:, 0].reshape(BO * ROWS, M), total[:, 1].reshape(BO * ROWS, M)], axis=1
        )
        hi, lo = split(total)
        value = jnp.dot(hi, alpha_hi[h], preferred_element_type=F32)
        value += jnp.dot(hi, alpha_lo[h], preferred_element_type=F32)
        value += jnp.dot(lo, alpha_hi[h], preferred_element_type=F32)
        return value

    across = lax.max(me - 1, 0) % 2
    middle = (me == 1) | (me == 2)
    other = me + 1 - 2 * across
    beyond = other + 1 - 2 * across

    def wait_block(block, c):
        hop(block, c, me // 3).wait_recv()

    def collect(c):
        wait_block(near, c)

        @pl.when(middle)
        def _():
            hop(near, c, across).start()
            wait_block(other, c)
            hop(other, c, 1 - across).start()

    def relay(c):
        @pl.when(middle)
        def _():
            wait_block(beyond, c)
            hop(beyond, c, 1 - across).start()

    def wait_second(i):
        @pl.when(jnp.logical_not(middle))
        def _():
            wait_block(second * 2, i)
            wait_block(second * 2 + 1, i)

    def own(i):
        select(i)
        if i == 0:
            pl.semaphore_wait(barrier, 4)
        send_own(i)

    def fetch_first(c):
        w_copy(first, c).start()

    def fetch_second():
        for c in range(CHUNKS):
            w_copy(second, c).start()

    def unit_first(c):
        w_copy(first, c).wait()
        unit(first, c * per, per, c == CHUNKS - 1)

    def unit_second(n):
        start, size, pieces = UNITS[n]
        for i in pieces:
            wait_second(i)
        if start % per == 0:
            w_copy(second, start // per).wait()
        unit(second, start, size, n == len(UNITS) - 1)

    def alpha_first():
        for blk in range(blocks):
            halfacc[blk] = alpha(first, blk)

    def stage(c):
        c_copy(c).start()

    acts = {
        "s": own, "c": collect, "r": relay, "f": fetch_first, "x": fetch_second, "p": prepare,
        "t": tables, "u": unit_first, "v": unit_second, "a": alpha_first, "k": stage,
    }
    for item in sum((part.split() for part in PLAN), []):
        acts[item[0]](*[int(item[1:])] if item[1:] else [])

    def x_copy(target, source, blk, off):
        return pltpu.make_async_remote_copy(
            src_ref=a_send.at[target, blk], dst_ref=a_recv.at[source, blk],
            send_sem=x_send_sem.at[off, blk], recv_sem=x_recv_sem.at[off, blk],
            device_id={"order": target}, device_id_type=MESH,
        )

    for c in range(len(PIECES)):
        @pl.when(me < 3)
        def _():
            hop(me, c, 0).wait_send()

        @pl.when(me > 0)
        def _():
            hop(me, c, 1).wait_send()

        @pl.when(middle)
        def _():
            hop(near, c, across).wait_send()
            hop(other, c, 1 - across).wait_send()
            hop(beyond, c, 1 - across).wait_send()

    for blk in range(blocks):
        value = (halfacc[blk] + alpha(second, blk)).astype(BF16)
        for t in range(4):
            a_send[t, blk] = value[:, t * M : (t + 1) * M]
        for off in (3, 2, 1):
            far = jnp.where(me < 2, (me + off) % 4, (me - off + 4) % 4)
            x_copy(far, me, blk, (far - me + 4) % 4).start()
        a_recv[me, blk] = a_send[me, blk]

    def gamma(source):
        rows = pl.ds(pl.multiple_of(source * P, P), P)
        got = [
            jnp.concatenate(
                [a_recv[source, blk, b * ROWS : (b + 1) * ROWS, :] for blk in range(blocks)], axis=0
            )
            for b in range(BO)
        ]
        parts = [
            jnp.concatenate([piece[:, x * P : (x + 1) * P] for piece in got], axis=1)
            for x in range(2)
        ]
        left = jnp.concatenate(parts + parts, axis=0)
        right = jnp.concatenate(
            [
                table[rows, x * SL : (x + 1) * SL]
                for table in (gamma_hi, gamma_lo)
                for x in range(2)
            ],
            axis=0,
        )
        score = lax.dot_general(left, right, dims, preferred_element_type=F32)
        return score.reshape(BO, P, SL)

    out_ref[0] = gamma(me)
    for off in (1, 2, 3):
        source = jnp.where(me < 2, (me + off) % 4, (me - off + 4) % 4)
        if off == 3:
            for blk in range(blocks):
                for away in (1, 2, 3):
                    x_copy((me + away) % 4, me, blk, away).wait_send()
                r_copy(first, blk).wait_send()
                r_copy(second, blk).wait_send()
        for blk in range(blocks):
            x_copy(source, source, blk, (me - source + 4) % 4).wait_recv()
        if off < 3:
            out_ref[0] += gamma(source)
        else:
            last_ref[0] = gamma(source)


def fused_shards(scene_coeffs, site_ids, gripper_coeffs, order_table, wigner):
    L, NBETA, P, SL = wigner.shape
    M = SL // 2
    K = 2 * scene_coeffs.shape[1]
    BO = NBETA // 2
    NB = P // ROWS
    cand = scene_coeffs.shape[4]
    tall = jnp.transpose(scene_coeffs, (0, 1, 2, 4, 3))
    tall = tall.reshape(K, 2, L // 2, cand // GROUP, GROUP, P)
    vmem = pl.BlockSpec(memory_space=pltpu.VMEM)
    hbm = pl.BlockSpec(memory_space=pltpu.HBM)
    score, last = pl.pallas_call(
        fused_kernel,
        out_shape=[jax.ShapeDtypeStruct((1, BO, P, SL), F32)] * 2,
        in_specs=[hbm, pl.BlockSpec(memory_space=pltpu.SMEM), hbm, hbm, hbm],
        out_specs=[vmem, vmem],
        scratch_shapes=[
            pltpu.VMEM((2, 2, L // 2, NBETA, P, M), BF16),
            *[
                pltpu.VMEM((K, 2, size, cand // GROUP, GROUP, P), BF16) for size in PIECES
            ],
            pltpu.VMEM((2, K // 2, L, P), BF16),
            pltpu.VMEM((2, 1, M), jnp.int32),
            pltpu.VMEM((4, L // 2, K, 2 * P), BF16),
            pltpu.VMEM((2, L // 2 // CHUNKS, 2 * P, M), BF16),
            pltpu.VMEM((2, NB, NBETA, 2, ROWS, M), F32),
            pltpu.VMEM((2, NB, BO, 2, ROWS, M), BF16),
            pltpu.VMEM((2, NB, BO, 2, ROWS, M), BF16),
            pltpu.VMEM((4, NB, BO * ROWS, M), BF16),
            pltpu.VMEM((4, NB, BO * ROWS, M), BF16),
            pltpu.VMEM((NB, BO * ROWS, 2 * SL), F32),
            pltpu.VMEM((2, 2 * M, 2 * SL), BF16),
            pltpu.VMEM((2, 2 * M, 2 * SL), BF16),
            pltpu.VMEM((SL, 2 * SL), BF16),
            pltpu.VMEM((SL, 2 * SL), BF16),
            pltpu.VMEM((K * L, 2 * P), F32),
            pltpu.VMEM((SL, M), jnp.int32),
            pltpu.SemaphoreType.DMA((2,)),
            pltpu.SemaphoreType.DMA((len(PIECES),)),
            pltpu.SemaphoreType.DMA((2, CHUNKS)),
            pltpu.SemaphoreType.DMA((2, 4, len(PIECES))),
            pltpu.SemaphoreType.DMA((4, len(PIECES))),
            pltpu.SemaphoreType.DMA((2, NB)),
            pltpu.SemaphoreType.DMA((2, NB)),
            pltpu.SemaphoreType.DMA((4, NB)),
            pltpu.SemaphoreType.DMA((4, NB)),
        ],
        compiler_params=pltpu.CompilerParams(
            collective_id=0, has_side_effects=True, vmem_limit_bytes=48 * 1024 * 1024
        ),
    )(
        tall,
        site_ids,
        pltpu.with_memory_space_constraint(gripper_coeffs, pltpu.HBM),
        pltpu.with_memory_space_constraint(order_table.reshape(2, 1, M), pltpu.HBM),
        wigner.reshape(2, L // 2, NBETA, P, SL),
    )
    return score + last


def solution(mesh):
    fits = mesh.shape["order"] == 4 and mesh.shape["degree"] == 2 and mesh.shape["site"] == 4
    shards = fused_shards if fits else general_shards
    in_specs = (
        P(None, None, "degree", "order", None),
        P("site"),
        P(None, None, "degree", "order"),
        P(),
        P("degree", None, "order", None),
    )
    out_specs = P("site", "degree", "order", None)
    return jax.shard_map(shards, mesh=mesh, in_specs=in_specs, out_specs=out_specs, check_vma=False)
```
